32 devices in a mesh: groups: 2 (over x), ctx: 16 (over z, y, core).
Axes of the slice: x: 2, y: 2, z: 4, core: 2. Of those that a mesh axis runs over, the one named last changes fastest.
Arguments:
- hidden_in: bfloat16 [32, 8192], P('groups', 'ctx'), parts along dimension 0, may hold values from -6 to 6
- attn_gain: float32 [8192], replicated, may hold values from 0.1 to 1.9
- w_query: bfloat16 [8192, 4096], P(None, 'ctx'), may hold values from -0.0625 to 0.0625
- w_key: bfloat16 [8192, 512], P(None, 'ctx'), may hold values from -0.375 to 0.375
- w_value: bfloat16 [8192, 512], P(None, 'ctx'), may hold values from -0.0625 to 0.0625
- rotated_prefix_keys: bfloat16 [32768, 4, 128], P(('groups', 'ctx')), parts along dimension 0, may hold values from -70 to 70
- cache_values: bfloat16 [32768, 4, 128], P(('groups', 'ctx')), parts along dimension 0, may hold values from -6 to 6
- w_out: bfloat16 [4096, 8192], P(None, 'ctx'), may hold values from -0.09375 to 0.09375
- ffn_gain: float32 [8192], replicated, may hold values from 0.1 to 1.9
- w_gate: bfloat16 [8192, 14336], P(None, 'ctx'), may hold values from -0.0625 to 0.0625
- w_up: bfloat16 [8192, 14336], P(None, 'ctx'), may hold values from -0.0625 to 0.0625
- w_down: bfloat16 [14336, 8192], P(None, 'ctx'), may hold values from -0.046875 to 0.046875
- doc_offsets: int32 [32], P('groups'), parts along dimension 0, may hold values from 8192 to 16384
- slot_request: int32 [32], P('groups'), parts along dimension 0, may hold values from 0 to 15, each once
Outputs:
- layer_out: bfloat16 [32, 8192], P('groups', 'ctx'), parts along dimension 0
The draws below stay inside these ranges and needn't reach their ends.
There are 2 independent parts, one for each index of `groups`. The reference program is written for one: setup_inputs(seed, part) draws one part's arguments, and reference() takes and returns one part's arrays. A program takes and returns all parts, laid end to end along the dimension named above; an argument that names none is the same for every part. Nothing has to cross between parts.
Inputs may be any that keep to these rules, and one draw needn't show every extreme that they name: `slot_request`: each slot holds a different request.
All inputs are finite; a program needn't handle non-finite values.
Results may differ from the reference program's by a relative error of at most 0.011.
Values may be sent and summed in bfloat16 or wider, within the bound.
No kernel may reach another device: no remote copies, remote signals or barrier semaphores. Data moves between devices by JAX's collectives and lax.ppermute only.
A program may use at most 128 MiB of HBM per device.

```python
import jax
import jax.numpy as jnp
from jax import lax

D = 8192
H = 32
KVH = 4
DH = 128
FF = 14336
Q = 16
CTX_DEV = 1024
CTX = 16384


def draw_rotated_prefix_keys(key, part):
    base_key = jax.random.fold_in(jax.random.fold_in(key, 17), 0)
    shape_full = (CTX, KVH, DH)
    drawn = jnp.clip(3.0 * jax.random.normal(base_key, shape_full, jnp.float32), -24.0, 24.0)
    return drawn.astype(jnp.bfloat16)


def touch_ends(result, rng, smallest, largest):
    place = [jax.random.randint(jax.random.fold_in(rng, axis), (), 0, length) for axis, length in enumerate(result.shape)]
    widest = result.shape.index(max(result.shape))
    neighbour = place[:widest] + [(place[widest] + 1) % result.shape[widest]] + place[widest + 1:]
    return result.at[tuple(place)].set(smallest).at[tuple(neighbour)].set(largest)


def steps_of(rng, dims, pieces, least, high):
    def one(dim, shards_of):
        draws = jax.random.uniform(jax.random.fold_in(jax.random.fold_in(rng, 6), dim), (shards_of,), jnp.float32, least / len(pieces), high / len(pieces))
        return jnp.repeat(jnp.exp(draws), dims[dim] // shards_of).reshape((-1,) + (1,) * (len(dims) - dim - 1))

    loudness = one(*pieces[0])
    for cut in pieces[1:]:
        loudness = loudness * one(*cut)
    return loudness


def normal_values(rng, shape, scale, limit, pieces=(), held_as=jnp.bfloat16):
    values = scale * jax.random.normal(rng, shape, jnp.float32)
    if pieces:
        values = values * steps_of(rng, shape, pieces, -0.22, 0.18)
    return jnp.clip(values, -limit, limit).astype(held_as)


def setup_inputs(seed: int = 0, part: int = 0) -> dict:
    arg_keys = jax.random.split(jax.random.key(seed), 15)
    part_keys = jax.random.split(jax.random.fold_in(arg_keys[14], part), 15)
    hidden_in = normal_values(part_keys[0], (Q, D), 1.0, 6.0, ((1, 16),))
    attn_gain = jnp.clip(1.0 + 0.18 * jax.random.normal(arg_keys[1], (D,), jnp.float32), 0.1, 1.9)
    w_query = normal_values(arg_keys[2], (D, H * DH), D ** -0.5, 0.0625, ((1, 16),))
    w_key = normal_values(arg_keys[3], (D, KVH * DH), (D // 36) ** -0.5, 0.375, ((1, 16),))
    w_value = normal_values(arg_keys[4], (D, KVH * DH), D ** -0.5, 0.0625, ((1, 16),))
    rotated_prefix_keys = draw_rotated_prefix_keys(jax.random.fold_in(jax.random.fold_in(arg_keys[14], part), 71), part)
    cache_values = normal_values(part_keys[6], (CTX, KVH, DH), 1.0, 6.0, ((0, 16),))
    w_out = normal_values(arg_keys[7], (H * DH, D), (H * DH) ** -0.5, 0.09375, ((1, 16),))
    ffn_gain = jnp.clip(1.0 + 0.18 * jax.random.normal(arg_keys[8], (D,), jnp.float32), 0.1, 1.9)
    w_gate = normal_values(arg_keys[9], (D, FF), D ** -0.5, 0.0625, ((1, 16),))
    w_up = normal_values(arg_keys[10], (D, FF), D ** -0.5, 0.0625, ((1, 16),))
    w_down = normal_values(arg_keys[11], (FF, D), FF ** -0.5, 0.046875, ((1, 16),))
    doc_offsets = touch_ends(jax.random.randint(part_keys[12], (Q,), CTX // 2, CTX + 1), jax.random.fold_in(part_keys[12], 1), CTX // 2, CTX).astype(jnp.int32)
    slot_request = jax.random.permutation(part_keys[13], Q).astype(jnp.int32)
    return {"hidden_in": hidden_in, "attn_gain": attn_gain, "w_query": w_query, "w_key": w_key, "w_value": w_value, "rotated_prefix_keys": rotated_prefix_keys, "cache_values": cache_values, "w_out": w_out, "ffn_gain": ffn_gain, "w_gate": w_gate, "w_up": w_up, "w_down": w_down, "doc_offsets": doc_offsets, "slot_request": slot_request}


NORM_EPSILON = 1e-05
ROPE_BASE = 500000.0
MASKED = -1e+30

def rms_norm(values, gain_row):
    wide_rows = values.astype(jnp.float32)
    factor = lax.rsqrt(lax.optimization_barrier(jnp.mean(wide_rows * wide_rows, axis=1, keepdims=True)) + NORM_EPSILON)
    return (wide_rows * factor * gain_row[None, :]).astype(jnp.bfloat16)

def rotate(columns, first_col, positions, head_dim):
    col_count = columns.shape[1]
    pair_cols = first_col + jnp.arange(col_count // 2, dtype=jnp.int32) * 2
    in_head = (pair_cols % head_dim).astype(jnp.float32)
    frequency = jnp.exp(-(in_head / head_dim) * jnp.log(jnp.float32(ROPE_BASE)))
    angles = positions.astype(jnp.float32)[:, None] * frequency[None, :]
    paired = columns.reshape(columns.shape[0], col_count // 2, 2)
    even_part = paired[..., 0]
    odd_part = paired[..., 1]
    cosine = jnp.cos(angles)
    sine = jnp.sin(angles)
    turned = jnp.stack([even_part * cosine - odd_part * sine, even_part * sine + odd_part * cosine], axis=-1)
    return turned.reshape(columns.shape)

def reference(hidden_in, attn_gain, w_query, w_key, w_value, rotated_prefix_keys, cache_values, w_out, ffn_gain, w_gate, w_up, w_down, doc_offsets, slot_request):
    batch_rows = hidden_in.shape[0]
    group_size = H // KVH
    logit_scale_factor = 1.0 / DH ** 0.5
    slot_index = jnp.arange(batch_rows, dtype=jnp.int32)
    positions = lax.optimization_barrier(jnp.sum(jnp.where(slot_request[:, None] == slot_index[None, :], doc_offsets[None, :], 0), axis=1)).astype(jnp.int32)
    normed = rms_norm(hidden_in, attn_gain)
    zero_col = jnp.int32(0)
    queries = rotate(jnp.dot(normed, w_query, preferred_element_type=jnp.float32), zero_col, positions, DH).astype(jnp.bfloat16)
    key_new = rotate(jnp.dot(normed, w_key, preferred_element_type=jnp.float32), zero_col, positions, DH).astype(jnp.bfloat16)
    value_new = jnp.dot(normed, w_value, preferred_element_type=jnp.float32).astype(jnp.bfloat16)
    query_groups = queries.astype(jnp.float32).reshape(batch_rows, KVH, group_size, DH)
    block_count = CTX // CTX_DEV
    keys_blocks = rotated_prefix_keys.reshape(block_count, CTX_DEV, KVH, DH)
    values_blocks = cache_values.reshape(block_count, CTX_DEV, KVH, DH)

    def visit(running, inputs):
        run_top, run_total, run_accum = running
        block_index, prefix_block_keys, prefix_block_values = inputs
        attention_logits = jnp.einsum('owqa,zwa->owqz', query_groups, prefix_block_keys.astype(jnp.float32)) * logit_scale_factor
        places = block_index * CTX_DEV + jnp.arange(CTX_DEV, dtype=jnp.int32)
        visible = (places[None, :] < positions[:, None])[:, None, None, :]
        masked = jnp.where(visible, attention_logits, MASKED)
        block_top = lax.optimization_barrier(jnp.max(masked, axis=3))
        weights = jnp.where(visible, jnp.exp(masked - block_top[..., None]), 0.0)
        block_total = lax.optimization_barrier(jnp.sum(weights, axis=3))
        rounded_attention_weights = lax.optimization_barrier(weights.astype(jnp.bfloat16))
        block_value_sum = jnp.einsum('nelw,weh->nelh', rounded_attention_weights.astype(jnp.float32), prefix_block_values.astype(jnp.float32))
        peak_score = jnp.maximum(run_top, block_top)
        old_share = jnp.exp(run_top - peak_score)
        new_share = jnp.exp(block_top - peak_score)
        merged_total = run_total * old_share + block_total * new_share
        merged_accum = run_accum * old_share[..., None] + block_value_sum * new_share[..., None]
        return ((peak_score, merged_total, merged_accum), None)
    start_state = (jnp.full((batch_rows, KVH, group_size), MASKED, jnp.float32), jnp.zeros((batch_rows, KVH, group_size), jnp.float32), jnp.zeros((batch_rows, KVH, group_size, DH), jnp.float32))
    (global_top, global_total, prefix_accum), _ = lax.scan(visit, start_state, (jnp.arange(block_count, dtype=jnp.int32), keys_blocks, values_blocks))
    own_score = jnp.einsum('rkgd,rkd->rkg', query_groups, key_new.astype(jnp.float32).reshape(batch_rows, KVH, DH)) * logit_scale_factor
    peak_score = jnp.maximum(global_top, own_score)
    kept_share = jnp.exp(global_top - peak_score)
    fresh_share = jnp.exp(own_score - peak_score)
    denominator = global_total * kept_share + fresh_share
    spread_value = value_new.astype(jnp.float32).reshape(batch_rows, KVH, 1, DH)
    attn_rows = (prefix_accum * kept_share[..., None] + fresh_share[..., None] * spread_value) / denominator[..., None]
    attn_rows = attn_rows.reshape(batch_rows, H * DH).astype(jnp.bfloat16)
    attn_full = jnp.dot(attn_rows, w_out, preferred_element_type=jnp.float32)
    residual_mid = (hidden_in.astype(jnp.float32) + attn_full).astype(jnp.bfloat16)
    normed_mid = rms_norm(residual_mid, ffn_gain)
    gate_act = jnp.dot(normed_mid, w_gate, preferred_element_type=jnp.float32)
    up_act = jnp.dot(normed_mid, w_up, preferred_element_type=jnp.float32)
    hidden = (jax.nn.silu(gate_act) * up_act).astype(jnp.bfloat16)
    layer_out = (residual_mid.astype(jnp.float32) + jnp.dot(hidden, w_down, preferred_element_type=jnp.float32)).astype(jnp.bfloat16)
    return layer_out
```

```python
import math

import jax
import jax.numpy as jnp
from jax import lax
from jax.experimental import pallas as pl
from jax.experimental.pallas import tpu as pltpu
from jax.sharding import PartitionSpec as P

NORM_EPSILON = 1e-05
ROPE_BASE = 500000.0
MASKED = -1e30


LANES = 128
VMEM = pl.BlockSpec(memory_space=pltpu.VMEM)


def exchange(blocks):
    return lax.all_to_all(blocks, "ctx", 0, 0)


def call(body, name, out_shape, args, scratch=(), flops=0):
    moved = sum(a.size * a.dtype.itemsize for a in args)
    return pl.pallas_call(
        body,
        out_shape=out_shape,
        in_specs=[VMEM] * len(args),
        out_specs=jax.tree.map(lambda _: VMEM, out_shape),
        scratch_shapes=list(scratch),
        compiler_params=pltpu.CompilerParams(vmem_limit_bytes=6 << 20),
        cost_estimate=pl.CostEstimate(flops=flops, bytes_accessed=moved, transcendentals=0),
        name=name,
    )(*args)


def norm_factor(blocks_ref):
    devices, rows, width = blocks_ref.shape

    def add(index, total):
        wide = blocks_ref[index].astype(jnp.float32)
        return total + wide * wide

    total = lax.fori_loop(0, devices, add, jnp.zeros((rows, width), jnp.float32), unroll=4)
    mean = jnp.sum(total, axis=1, keepdims=True) / (devices * width)
    return lax.rsqrt(mean + NORM_EPSILON)


def normed_block(blocks_ref, gain_ref, factor, index):
    wide = blocks_ref[index].astype(jnp.float32)
    return (wide * factor * gain_ref[index]).astype(jnp.bfloat16)


def products(devices, depth, block_of, weight_refs, total_refs):
    for total_ref in total_refs:
        total_ref[...] = jnp.zeros_like(total_ref)

    def step(index, carry):
        block = block_of(index)
        span = pl.ds(pl.multiple_of(index * depth, depth), depth)
        for weight_ref, total_ref in zip(weight_refs, total_refs):
            total_ref[...] += jnp.dot(
                block, weight_ref[span, :], preferred_element_type=jnp.float32
            )
        return carry

    lax.fori_loop(0, devices, step, 0, unroll=4)


def project_kernel(
    blocks_ref, gain_ref, query_ref, key_ref, value_ref, cos_ref, sin_ref, out_ref,
    query_total, key_total, value_total, joined,
):
    devices, _, depth = blocks_ref.shape
    factor = norm_factor(blocks_ref)
    products(
        devices, depth,
        lambda index: normed_block(blocks_ref, gain_ref, factor, index),
        (query_ref, key_ref, value_ref),
        (query_total, key_total, value_total),
    )
    query_width = query_total.shape[1]
    key_width = key_total.shape[1]
    used = query_width + 2 * key_width
    joined[...] = jnp.zeros_like(joined)
    joined[:, :query_width] = query_total[...]
    joined[:, query_width : query_width + key_width] = key_total[...]
    joined[:, query_width + key_width : used] = value_total[...]
    columns = joined[...]
    width = columns.shape[1]
    lane = lax.broadcasted_iota(jnp.int32, columns.shape, 1)
    partner = jnp.where(
        lane % 2 == 1, pltpu.roll(columns, 1, 1), -pltpu.roll(columns, width - 1, 1)
    )
    turned = columns * cos_ref[...] + partner * sin_ref[...]
    sent = turned.astype(jnp.bfloat16)[:, :used]

    def put(index, carry):
        out_ref[index] = sent
        return carry

    lax.fori_loop(0, devices, put, 0, unroll=4)


def attend_kernel(scale, query_ref, key_ref, value_ref, limit_ref, out_ref):
    heads, rows, head_dim = query_ref.shape
    span = key_ref.shape[0]
    value_heads = key_ref.shape[1] // head_dim
    group = heads // value_heads
    devices = out_ref.shape[0]
    pairs = heads * rows // devices
    place = lax.broadcasted_iota(jnp.int32, (rows, span), 1)
    visible = (place < limit_ref[...])[None]
    for g in range(value_heads):
        lanes = pl.ds(g * head_dim, head_dim)
        queries = query_ref[g * group : (g + 1) * group].reshape(group * rows, head_dim)
        logits = lax.dot_general(
            queries, key_ref[:, lanes], (((1,), (1,)), ((), ())),
            preferred_element_type=jnp.float32,
        ) * scale
        masked = jnp.where(visible, logits.reshape(group, rows, span), MASKED)
        top = jnp.max(masked, axis=2, keepdims=True)
        weights = jnp.where(visible, jnp.exp(masked - top), 0.0)
        total = jnp.sum(weights, axis=2, keepdims=True).reshape(group * rows, 1)
        top = top.reshape(group * rows, 1)
        summed = jnp.dot(
            weights.astype(jnp.bfloat16).reshape(group * rows, span), value_ref[:, lanes],
            preferred_element_type=jnp.float32,
        )
        seen = total > 0.0
        safe = jnp.where(seen, total, 1.0)
        means = (summed / safe).astype(jnp.bfloat16)
        level = jnp.where(seen, top + jnp.log(safe), MASKED)
        across = jnp.transpose(jnp.broadcast_to(level, (group * rows, LANES)))[:8]
        for first in range(0, group * rows, LANES):
            line = across[:, first : first + LANES]
            high = line.astype(jnp.bfloat16)
            rest = line - high.astype(jnp.float32)
            middle = rest.astype(jnp.bfloat16)
            low = (rest - middle.astype(jnp.float32)).astype(jnp.bfloat16)
            row = lax.broadcasted_iota(jnp.int32, line.shape, 0)
            terms = jnp.where(
                row == 0,
                high.astype(jnp.float32),
                jnp.where(row == 1, middle.astype(jnp.float32), low.astype(jnp.float32)),
            ).astype(jnp.bfloat16)
            for begin in range(0, LANES, pairs):
                index = (g * group * rows + first + begin) // pairs
                out_ref[index, :pairs] = means[first + begin : first + begin + pairs]
                out_ref[index, pairs:] = terms


def output_kernel(blocks_ref, weight_ref, residual_ref, mid_ref, out_ref, total):
    heads, rows, head_dim = blocks_ref.shape
    devices = out_ref.shape[0]

    def block_of(index):
        return jnp.concatenate([blocks_ref[2 * index], blocks_ref[2 * index + 1]], axis=1)

    products(heads // 2, 2 * head_dim, block_of, (weight_ref,), (total,))
    mid = (residual_ref[...].astype(jnp.float32) + total[...]).astype(jnp.bfloat16)
    mid_ref[...] = mid

    def put(index, carry):
        out_ref[index] = mid
        return carry

    lax.fori_loop(0, devices, put, 0, unroll=4)


def gated_kernel(blocks_ref, gain_ref, gate_ref, up_ref, out_ref, gate_total, up_total):
    devices, _, depth = blocks_ref.shape
    factor = norm_factor(blocks_ref)
    products(
        devices, depth,
        lambda index: normed_block(blocks_ref, gain_ref, factor, index),
        (gate_ref, up_ref),
        (gate_total, up_total),
    )
    gate = gate_total[...]
    hidden = (gate / (1.0 + jnp.exp(-gate)) * up_total[...]).astype(jnp.bfloat16)

    def put(index, carry):
        out_ref[index] = hidden
        return carry

    lax.fori_loop(0, devices, put, 0, unroll=4)


def down_kernel(blocks_ref, weight_ref, residual_ref, out_ref, total):
    devices, _, depth = blocks_ref.shape
    products(devices, depth, lambda index: blocks_ref[index], (weight_ref,), (total,))
    out_ref[...] = (residual_ref[...].astype(jnp.float32) + total[...]).astype(jnp.bfloat16)


def rotation(first_col, width, positions, head_dim):
    col = jnp.arange(width, dtype=jnp.int32)
    in_head = ((first_col + col - col % 2) % head_dim).astype(jnp.float32)
    frequency = jnp.exp(-(in_head / head_dim) * jnp.log(jnp.float32(ROPE_BASE)))
    angles = positions.astype(jnp.float32)[:, None] * frequency[None, :]
    return jnp.cos(angles), jnp.sin(angles)


def shards(
    hidden_in,
    attn_gain,
    w_query,
    w_key,
    w_value,
    rotated_prefix_keys,
    cache_values,
    w_out,
    ffn_gain,
    w_gate,
    w_up,
    w_down,
    doc_offsets,
    slot_request,
):
    devices = lax.axis_size("ctx")
    device = lax.axis_index("ctx")
    rows, width = hidden_in.shape
    span, value_heads, head_dim = rotated_prefix_keys.shape
    query_width = w_query.shape[1]
    key_width = w_key.shape[1]
    heads = query_width * devices // head_dim
    group = heads // value_heads
    scale = 1.0 / math.sqrt(head_dim)
    slot_index = jnp.arange(rows, dtype=jnp.int32)
    positions = jnp.sum(
        jnp.where(slot_request[:, None] == slot_index[None, :], doc_offsets[None, :], 0), axis=1
    )

    def buffer(*shape, dtype=jnp.bfloat16):
        return jax.ShapeDtypeStruct(shape, dtype)

    def totals(*widths):
        return [pltpu.VMEM((rows, w), jnp.float32) for w in widths]

    used = query_width + 2 * key_width
    padded = -(-used // LANES) * LANES
    query_cos, query_sin = rotation(device * query_width, query_width, positions, head_dim)
    key_cos, key_sin = rotation(device * key_width, key_width, positions, head_dim)
    still = jnp.ones((rows, padded - query_width - key_width), jnp.float32)
    cosine = jnp.concatenate([query_cos, key_cos, still], axis=1)
    sine = jnp.concatenate([query_sin, key_sin, still * 0.0], axis=1)
    full = exchange(jnp.broadcast_to(hidden_in[None], (devices, rows, width)))
    packed = exchange(
        call(
            project_kernel, "project", buffer(devices, rows, used),
            (full, attn_gain.reshape(devices, 1, width), w_query, w_key, w_value, cosine, sine),
            totals(query_width, key_width, key_width, padded),
            2 * rows * devices * width * used,
        )
    )

    def unpacked(first, part_width):
        part = packed[:, :, first : first + part_width]
        if part_width >= head_dim:
            split = part.reshape(devices, rows, part_width // head_dim, head_dim)
            return split.transpose(0, 2, 1, 3).reshape(-1, rows, head_dim)
        run = head_dim // part_width
        return part.reshape(-1, run, rows, part_width).transpose(0, 2, 1, 3).reshape(
            -1, rows, head_dim
        )

    queries = unpacked(0, query_width)
    key_new = unpacked(query_width, key_width)
    value_new = unpacked(query_width + key_width, key_width)
    pairs = heads * rows // devices
    limit = (positions - device * span)[:, None]
    sent = call(
        lambda *refs: attend_kernel(scale, *refs), "attend", buffer(devices, pairs + 8, LANES),
        (
            queries,
            rotated_prefix_keys.reshape(span, value_heads * head_dim),
            cache_values.reshape(span, value_heads * head_dim),
            limit,
        ),
        (),
        4 * heads * rows * span * head_dim,
    )
    got = exchange(sent)
    first_pair = device * pairs
    means = got[:, :pairs].astype(jnp.float32)
    terms = lax.dynamic_slice_in_dim(
        got[:, pairs : pairs + 3].astype(jnp.float32), first_pair % LANES, pairs, 2
    )
    levels = terms[:, 0] + terms[:, 1] + terms[:, 2]

    def mine(every):
        return lax.dynamic_slice_in_dim(
            every.reshape(heads * rows, head_dim), first_pair, pairs, 0
        ).astype(jnp.float32)

    def spread(new):
        return jnp.broadcast_to(new[:, None], (value_heads, group, rows, head_dim))

    own_score = jnp.sum(mine(queries) * mine(spread(key_new)), axis=1) * scale
    own_value = mine(spread(value_new))
    peak = jnp.maximum(jnp.max(levels, axis=0), own_score)
    shares = jnp.exp(levels - peak[None, :])
    own_share = jnp.exp(own_score - peak)
    numerator = jnp.sum(shares[..., None] * means, axis=0) + own_share[:, None] * own_value
    denominator = jnp.sum(shares, axis=0) + own_share
    attn_part = (numerator / denominator[:, None]).astype(jnp.bfloat16)
    attn_all = exchange(jnp.broadcast_to(attn_part[None], (devices, pairs, head_dim)))
    mid_part, mid_sent = call(
        output_kernel, "output", (buffer(rows, width), buffer(devices, rows, width)),
        (attn_all.reshape(heads, rows, head_dim), w_out, hidden_in),
        totals(width),
        2 * rows * heads * head_dim * width,
    )
    hidden_width = w_gate.shape[1]
    hidden_sent = call(
        gated_kernel, "gated", buffer(devices, rows, hidden_width),
        (exchange(mid_sent), ffn_gain.reshape(devices, 1, width), w_gate, w_up),
        totals(hidden_width, hidden_width),
        4 * rows * devices * width * hidden_width,
    )
    return call(
        down_kernel, "down", buffer(rows, width),
        (exchange(hidden_sent), w_down, mid_part),
        totals(width),
        2 * rows * devices * hidden_width * width,
    )


def solution(mesh):
    return jax.shard_map(
        shards,
        mesh=mesh,
        in_specs=(
            P("groups", "ctx"),
            P(),
            P(None, "ctx"),
            P(None, "ctx"),
            P(None, "ctx"),
            P(("groups", "ctx"), None, None),
            P(("groups", "ctx"), None, None),
            P(None, "ctx"),
            P(),
            P(None, "ctx"),
            P(None, "ctx"),
            P(None, "ctx"),
            P("groups"),
            P("groups"),
        ),
        out_specs=P("groups", "ctx"),
        check_vma=False,
    )
```

```python
import math

import jax
import jax.numpy as jnp
from jax import lax
from jax.experimental import pallas as pl
from jax.experimental.pallas import tpu as pltpu
from jax.sharding import PartitionSpec as P

NORM_EPSILON = 1e-05
ROPE_BASE = 500000.0
MASKED = -1e30


LANES = 128
FLOPS = {"table": 10**11, "finish": 10**11, "output": 10**11}
VMEM = pl.BlockSpec(memory_space=pltpu.VMEM)
SMEM = pl.BlockSpec(memory_space=pltpu.SMEM)


def exchange(blocks):
    return lax.all_to_all(blocks, "ctx", 0, 0)


def digits(devices):
    rest, stride, place, out = devices // 2, devices, 1, []
    while rest > 1:
        radix = 4 if rest % 4 == 0 else 2
        stride //= radix
        out.append((stride, radix, place))
        place *= radix
        rest //= radix
    return out + [(1, 2, place)]


def mask_at(place_index, devices):
    return sum(((place_index // place) % radix) * stride for stride, radix, place in digits(devices))


def place_of(mask, devices):
    return sum(((mask // stride) % radix) * place for stride, radix, place in digits(devices))


def shifted(part, mask):
    devices = lax.axis_size("ctx")
    return lax.ppermute(part, "ctx", [(index, index ^ mask) for index in range(devices)])


def gathered(part):
    devices = lax.axis_size("ctx")
    held = part[None]
    for stride, radix, _ in digits(devices)[:-1]:
        held = jnp.concatenate(
            [held] + [shifted(held, stride * digit) for digit in range(1, radix)], axis=0
        )
    return held, shifted(held, 1)


def call(body, name, out_shape, args, scratch=(), flops=0):
    moved = sum(a.size * a.dtype.itemsize for a in args)
    return pl.pallas_call(
        body,
        out_shape=out_shape,
        in_specs=[SMEM if a.dtype == jnp.int32 and a.ndim == 1 else VMEM for a in args],
        out_specs=jax.tree.map(lambda _: VMEM, out_shape),
        scratch_shapes=list(scratch),
        compiler_params=pltpu.CompilerParams(vmem_limit_bytes=6 << 20),
        cost_estimate=pl.CostEstimate(flops=FLOPS.get(name, flops), bytes_accessed=moved, transcendentals=0),
        name=name,
    )(*args)


def norm_factor(halves):
    places, rows, width = halves[0].shape

    def add(index, total):
        for half in halves:
            wide = half[index].astype(jnp.float32)
            total = total + wide * wide
        return total

    total = lax.fori_loop(0, places, add, jnp.zeros((rows, width), jnp.float32), unroll=4)
    mean = jnp.sum(total, axis=1, keepdims=True) / (2 * places * width)
    return lax.rsqrt(mean + NORM_EPSILON)


def products(device_ref, halves, value_of, weight_refs, total_refs):
    places, _, depth = halves[0].shape
    for total_ref in total_refs:
        total_ref[...] = jnp.zeros_like(total_ref)

    def step(index, carry):
        for number, half in enumerate(halves):
            mask = mask_at(index, 2 * places) + number
            owner = lax.bitwise_xor(device_ref[0], mask)
            block = value_of(half[index], owner)
            span = pl.ds(pl.multiple_of(owner * depth, depth), depth)
            for weight_ref, total_ref in zip(weight_refs, total_refs):
                total_ref[...] += jnp.dot(
                    block, weight_ref[span, :], preferred_element_type=jnp.float32
                )
        return carry

    lax.fori_loop(0, places, step, 0, unroll=4)


def normed_products(device_ref, halves, gain_ref, weight_refs, total_refs):
    factor = norm_factor(halves)

    def normed(block, owner):
        return (block.astype(jnp.float32) * factor * gain_ref[owner]).astype(jnp.bfloat16)

    products(device_ref, halves, normed, weight_refs, total_refs)


def project_kernel(
    device_ref, near_ref, far_ref, gain_ref, query_ref, key_ref, value_ref, cos_ref, sin_ref,
    out_ref, query_total, key_total, value_total, joined,
):
    normed_products(
        device_ref, (near_ref, far_ref), gain_ref,
        (query_ref, key_ref, value_ref),
        (query_total, key_total, value_total),
    )
    query_width = query_total.shape[1]
    key_width = key_total.shape[1]
    used = query_width + 2 * key_width
    joined[...] = jnp.zeros_like(joined)
    joined[:, :query_width] = query_total[...]
    joined[:, query_width : query_width + key_width] = key_total[...]
    joined[:, query_width + key_width : used] = value_total[...]
    columns = joined[...]
    width = columns.shape[1]
    lane = lax.broadcasted_iota(jnp.int32, columns.shape, 1)
    partner = jnp.where(
        lane % 2 == 1, pltpu.roll(columns, 1, 1), pltpu.roll(columns, width - 1, 1)
    )
    turned = columns * cos_ref[...] + partner * sin_ref[...]
    out_ref[...] = turned.astype(jnp.bfloat16)[:, :used]


def attend_kernel(scale, query_ref, key_ref, value_ref, limit_ref, out_ref):
    heads, rows, head_dim = query_ref.shape
    span = key_ref.shape[0]
    value_heads = key_ref.shape[1] // head_dim
    group = heads // value_heads
    devices = out_ref.shape[0]
    pairs = heads * rows // devices
    place = lax.broadcasted_iota(jnp.int32, (rows, span), 1)
    visible = (place < limit_ref[...])[None]
    for g in range(value_heads):
        lanes = pl.ds(g * head_dim, head_dim)
        queries = query_ref[g * group : (g + 1) * group].reshape(group * rows, head_dim)
        logits = lax.dot_general(
            queries, key_ref[:, lanes], (((1,), (1,)), ((), ())),
            preferred_element_type=jnp.float32,
        ) * scale
        masked = jnp.where(visible, logits.reshape(group, rows, span), MASKED)
        top = jnp.max(masked, axis=2, keepdims=True)
        weights = jnp.where(visible, jnp.exp(masked - top), 0.0)
        total = jnp.sum(weights, axis=2, keepdims=True).reshape(group * rows, 1)
        top = top.reshape(group * rows, 1)
        summed = jnp.dot(
            weights.astype(jnp.bfloat16).reshape(group * rows, span), value_ref[:, lanes],
            preferred_element_type=jnp.float32,
        )
        seen = total > 0.0
        safe = jnp.where(seen, total, 1.0)
        means = (summed / safe).astype(jnp.bfloat16)
        level = jnp.where(seen, top + jnp.log(safe), MASKED)
        across = jnp.transpose(jnp.broadcast_to(level, (group * rows, LANES)))[:8]
        for first in range(0, group * rows, LANES):
            line = across[:, first : first + LANES]
            high = line.astype(jnp.bfloat16)
            rest = line - high.astype(jnp.float32)
            middle = rest.astype(jnp.bfloat16)
            low = (rest - middle.astype(jnp.float32)).astype(jnp.bfloat16)
            row = lax.broadcasted_iota(jnp.int32, line.shape, 0)
            terms = jnp.where(
                row == 0,
                high.astype(jnp.float32),
                jnp.where(row == 1, middle.astype(jnp.float32), low.astype(jnp.float32)),
            ).astype(jnp.bfloat16)
            for begin in range(0, LANES, pairs):
                index = (g * group * rows + first + begin) // pairs
                out_ref[index, :pairs] = means[first + begin : first + begin + pairs]
                out_ref[index, pairs:] = terms


def order_kernel(device_ref, held_ref, out_ref):
    devices = held_ref.shape[0]

    def move(owner, carry):
        place = place_of(lax.bitwise_xor(device_ref[0], owner), devices)
        out_ref[owner] = held_ref[place]
        return carry

    lax.fori_loop(0, devices, move, 0, unroll=4)


def table_kernel(cos_ref, sin_ref, cos_out_ref, sin_out_ref):
    lane = lax.broadcasted_iota(jnp.int32, sin_ref.shape, 1)
    cos_out_ref[...] = cos_ref[...]
    sin_out_ref[...] = jnp.where(lane % 2 == 1, sin_ref[...], -sin_ref[...])


def finish_kernel(numerator_ref, denominator_ref, out_ref):
    out_ref[...] = (numerator_ref[...] / denominator_ref[...]).astype(jnp.bfloat16)


def output_kernel(blocks_ref, weight_ref, residual_ref, mid_ref, total):
    heads, _, head_dim = blocks_ref.shape
    total[...] = jnp.zeros_like(total)

    def step(index, carry):
        block = jnp.concatenate([blocks_ref[2 * index], blocks_ref[2 * index + 1]], axis=1)
        span = pl.ds(pl.multiple_of(index * 2 * head_dim, head_dim), 2 * head_dim)
        total[...] += jnp.dot(block, weight_ref[span, :], preferred_element_type=jnp.float32)
        return carry

    lax.fori_loop(0, heads // 2, step, 0, unroll=4)
    mid_ref[...] = (residual_ref[...].astype(jnp.float32) + total[...]).astype(jnp.bfloat16)


def gated_kernel(
    device_ref, near_ref, far_ref, gain_ref, gate_ref, up_ref, out_ref, gate_total, up_total
):
    normed_products(
        device_ref, (near_ref, far_ref), gain_ref, (gate_ref, up_ref), (gate_total, up_total)
    )
    gate = gate_total[...]
    out_ref[...] = (gate / (1.0 + jnp.exp(-gate)) * up_total[...]).astype(jnp.bfloat16)


def down_kernel(device_ref, near_ref, far_ref, weight_ref, residual_ref, out_ref, total):
    products(device_ref, (near_ref, far_ref), lambda block, _: block, (weight_ref,), (total,))
    out_ref[...] = (residual_ref[...].astype(jnp.float32) + total[...]).astype(jnp.bfloat16)


def rotation(first_col, width, positions, head_dim):
    col = jnp.arange(width, dtype=jnp.int32)
    in_head = ((first_col + col - col % 2) % head_dim).astype(jnp.float32)
    frequency = jnp.exp(-(in_head / head_dim) * jnp.log(jnp.float32(ROPE_BASE)))
    angles = positions.astype(jnp.float32)[:, None] * frequency[None, :]
    return jnp.cos(angles), jnp.sin(angles)


def shards(
    hidden_in,
    attn_gain,
    w_query,
    w_key,
    w_value,
    rotated_prefix_keys,
    cache_values,
    w_out,
    ffn_gain,
    w_gate,
    w_up,
    w_down,
    doc_offsets,
    slot_request,
):
    devices = lax.axis_size("ctx")
    device = lax.axis_index("ctx")
    rows, width = hidden_in.shape
    span, value_heads, head_dim = rotated_prefix_keys.shape
    query_width = w_query.shape[1]
    key_width = w_key.shape[1]
    heads = query_width * devices // head_dim
    group = heads // value_heads
    scale = 1.0 / math.sqrt(head_dim)
    slot_index = jnp.arange(rows, dtype=jnp.int32)
    positions = jnp.sum(
        jnp.where(slot_request[:, None] == slot_index[None, :], doc_offsets[None, :], 0), axis=1
    )

    def buffer(*shape, dtype=jnp.bfloat16):
        return jax.ShapeDtypeStruct(shape, dtype)

    def totals(*widths):
        return [pltpu.VMEM((rows, w), jnp.float32) for w in widths]

    used = query_width + 2 * key_width
    padded = -(-used // LANES) * LANES
    query_cos, query_sin = rotation(device * query_width, query_width, positions, head_dim)
    key_cos, key_sin = rotation(device * key_width, key_width, positions, head_dim)
    still = jnp.ones((rows, padded - query_width - key_width), jnp.float32)
    cosine = jnp.concatenate([query_cos, key_cos, still], axis=1)
    sine = jnp.concatenate([query_sin, key_sin, still * 0.0], axis=1)
    table = buffer(rows, padded, dtype=jnp.float32)
    cosine, sine = call(table_kernel, "table", (table, table), (cosine, sine), (), FLOPS["table"])
    own = device.astype(jnp.int32)[None]
    projected = call(
        project_kernel, "project", buffer(rows, used),
        (
            own, *gathered(hidden_in), attn_gain.reshape(devices, 1, width),
            w_query, w_key, w_value, cosine, sine,
        ),
        totals(query_width, key_width, key_width, padded),
        2 * rows * devices * width * used,
    )
    packed = exchange(jnp.broadcast_to(projected[None], (devices, rows, used)))

    def unpacked(first, part_width):
        part = packed[:, :, first : first + part_width]
        if part_width >= head_dim:
            split = part.reshape(devices, rows, part_width // head_dim, head_dim)
            return split.transpose(0, 2, 1, 3).reshape(-1, rows, head_dim)
        run = head_dim // part_width
        return part.reshape(-1, run, rows, part_width).transpose(0, 2, 1, 3).reshape(
            -1, rows, head_dim
        )

    queries = unpacked(0, query_width)
    key_new = unpacked(query_width, key_width)
    value_new = unpacked(query_width + key_width, key_width)
    pairs = heads * rows // devices
    limit = (positions - device * span)[:, None]
    sent = call(
        lambda *refs: attend_kernel(scale, *refs), "attend", buffer(devices, pairs + 8, LANES),
        (
            queries,
            rotated_prefix_keys.reshape(span, value_heads * head_dim),
            cache_values.reshape(span, value_heads * head_dim),
            limit,
        ),
        (),
        4 * heads * rows * span * head_dim,
    )
    got = exchange(sent)
    first_pair = device * pairs
    means = got[:, :pairs].astype(jnp.float32)
    terms = lax.dynamic_slice_in_dim(
        got[:, pairs : pairs + 3].astype(jnp.float32), first_pair % LANES, pairs, 2
    )
    levels = terms[:, 0] + terms[:, 1] + terms[:, 2]

    def mine(every):
        return lax.dynamic_slice_in_dim(
            every.reshape(heads * rows, head_dim), first_pair, pairs, 0
        ).astype(jnp.float32)

    def spread(new):
        return jnp.broadcast_to(new[:, None], (value_heads, group, rows, head_dim))

    own_score = jnp.sum(mine(queries) * mine(spread(key_new)), axis=1) * scale
    own_value = mine(spread(value_new))
    peak = jnp.maximum(jnp.max(levels, axis=0), own_score)
    shares = jnp.exp(levels - peak[None, :])
    own_share = jnp.exp(own_score - peak)
    numerator = jnp.sum(shares[..., None] * means, axis=0) + own_share[:, None] * own_value
    denominator = jnp.sum(shares, axis=0) + own_share
    attn_part = call(
        finish_kernel, "finish", buffer(pairs, head_dim), (numerator, denominator[:, None]), (),
        FLOPS["finish"],
    )
    held = jnp.concatenate(gathered(attn_part), axis=0)
    attn_all = call(
        order_kernel, "order", buffer(devices, pairs, head_dim), (own, held)
    )
    mid_part = call(
        output_kernel, "output", buffer(rows, width),
        (attn_all.reshape(heads, rows, head_dim), w_out, hidden_in),
        totals(width),
        2 * rows * heads * head_dim * width,
    )
    hidden_width = w_gate.shape[1]
    hidden = call(
        gated_kernel, "gated", buffer(rows, hidden_width),
        (own, *gathered(mid_part), ffn_gain.reshape(devices, 1, width), w_gate, w_up),
        totals(hidden_width, hidden_width),
        4 * rows * devices * width * hidden_width,
    )
    return call(
        down_kernel, "down", buffer(rows, width),
        (own, *gathered(hidden), w_down, mid_part),
        totals(width),
        2 * rows * devices * hidden_width * width,
    )


def solution(mesh):
    return jax.shard_map(
        shards,
        mesh=mesh,
        in_specs=(
            P("groups", "ctx"),
            P(),
            P(None, "ctx"),
            P(None, "ctx"),
            P(None, "ctx"),
            P(("groups", "ctx"), None, None),
            P(("groups", "ctx"), None, None),
            P(None, "ctx"),
            P(),
            P(None, "ctx"),
            P(None, "ctx"),
            P(None, "ctx"),
            P("groups"),
            P("groups"),
        ),
        out_specs=P("groups", "ctx"),
        check_vma=False,
    )
```

```python
import math

import jax
import jax.numpy as jnp
from jax import lax
from jax.experimental import pallas as pl
from jax.experimental.pallas import tpu as pltpu
from jax.sharding import PartitionSpec as P


NORM_EPSILON = 1e-05
ROPE_BASE = 500000.0
MASKED = -1e30


LANES = 128
FLOPS = {"begin": 10**11, "table": 10**11, "finish": 10**11, "output": 10**11, "relay": 10**11}
VMEM = pl.BlockSpec(memory_space=pltpu.VMEM)
SMEM = pl.BlockSpec(memory_space=pltpu.SMEM)


def exchange(blocks):
    return lax.all_to_all(blocks, "ctx", 0, 0)


def digits(devices):
    rest, stride, place, out = devices // 2, devices, 1, []
    while rest > 1:
        radix = 4 if rest % 4 == 0 else 2
        stride //= radix
        out.append((stride, radix, place))
        place *= radix
        rest //= radix
    return out + [(1, 2, place)]


def mask_at(place_index, devices):
    return sum(((place_index // place) % radix) * stride for stride, radix, place in digits(devices))


def place_of(mask, devices):
    return sum(((mask // stride) % radix) * place for stride, radix, place in digits(devices))


def shifted(part, mask):
    devices = lax.axis_size("ctx")
    return lax.ppermute(part, "ctx", [(index, index ^ mask) for index in range(devices)])


def gathered(part):
    devices = lax.axis_size("ctx")
    held = part[None]
    *rounds, last, _ = digits(devices)

    def arrive(stride, radix):
        return [shifted(held, stride * digit) for digit in range(1, radix)]

    for stride, radix, _ in rounds:
        held = jnp.concatenate([held] + arrive(stride, radix), axis=0)
    brought = arrive(*last[:2])
    near = jnp.concatenate([held] + brought, axis=0)
    return held, brought, shifted(near, 1)


def together(pieces):
    held, brought, far = pieces
    return jnp.concatenate([held, *brought, far], axis=0)


def call(body, name, out_shape, args, scratch=(), flops=0):
    moved = sum(a.size * a.dtype.itemsize for a in args)
    return pl.pallas_call(
        body,
        out_shape=out_shape,
        in_specs=[SMEM if a.dtype == jnp.int32 and a.ndim == 1 else VMEM for a in args],
        out_specs=jax.tree.map(lambda _: VMEM, out_shape),
        scratch_shapes=list(scratch),
        compiler_params=pltpu.CompilerParams(vmem_limit_bytes=6 << 20),
        cost_estimate=pl.CostEstimate(flops=FLOPS.get(name, flops), bytes_accessed=moved, transcendentals=0),
    )(*args)


def accumulate(device_ref, devices, pieces, gain_ref, weight_refs, total_refs, square_ref):
    for first, piece_ref in pieces:
        places, _, depth = piece_ref.shape

        def step(index, carry):
            owner = lax.bitwise_xor(device_ref[0], mask_at(first + index, devices))
            block = piece_ref[index]
            if gain_ref is not None:
                wide = block.astype(jnp.float32)
                block = (wide * gain_ref[owner]).astype(jnp.bfloat16)
                square_ref[...] += sum(
                    wide[:, lane : lane + LANES] * wide[:, lane : lane + LANES]
                    for lane in range(0, depth, LANES)
                ) if depth % LANES == 0 else jnp.broadcast_to(
                    jnp.sum(wide * wide, axis=1, keepdims=True) / LANES, square_ref.shape
                )
            span = pl.ds(pl.multiple_of(owner * depth, depth), depth)
            for weight_ref, total_ref in zip(weight_refs, total_refs):
                if weight_ref.shape[1] == devices * depth:
                    total_ref[...] += lax.dot_general(
                        block, weight_ref[:, span], (((1,), (1,)), ((), ())),
                        preferred_element_type=jnp.float32,
                    )
                else:
                    total_ref[...] += jnp.dot(
                        block, weight_ref[span, :], preferred_element_type=jnp.float32
                    )
            return carry

        lax.fori_loop(0, places, step, 0, unroll=4)


def contract(name, pieces, own, weights, widths, gain, finish, extras, out_shape):
    held, brought, far = pieces
    devices = lax.axis_size("ctx")
    _, rows, depth = held.shape
    normed = gain is not None
    gains = [gain.reshape(devices, 1, depth)] if normed else []
    totals_of = [jax.ShapeDtypeStruct((rows, w), jnp.float32) for w in widths]
    if normed:
        totals_of.append(jax.ShapeDtypeStruct((rows, LANES), jnp.float32))
    scratch = [pltpu.VMEM(t.shape, t.dtype) for t in totals_of]

    def stage(label, first, parts, before, last):
        def kernel(device_ref, *refs):
            refs = list(refs)
            take = lambda count: [refs.pop(0) for _ in range(count)]
            part_refs, gain_refs, weight_refs = take(len(parts)), take(len(gains)), take(len(weights))
            before_refs = take(len(before))
            extra_refs = take(len(extras)) if last else []
            out_refs = take(1 if last else 0)
            total_refs = refs
            for index, total_ref in enumerate(total_refs):
                if before:
                    total_ref[...] = before_refs[index][...]
                else:
                    total_ref[...] = jnp.zeros_like(total_ref)
            place, placed = first, []
            for part_ref in part_refs:
                placed.append((place, part_ref))
                place += part_ref.shape[0]
            accumulate(
                device_ref, devices, placed, gain_refs[0] if normed else None,
                weight_refs, total_refs[: len(weights)], total_refs[-1],
            )
            if last:
                factor = None
                if normed:
                    mean = jnp.sum(total_refs[-1][...], axis=1, keepdims=True) / (devices * depth)
                    factor = lax.rsqrt(mean + NORM_EPSILON)
                finish(factor, [t[...] for t in total_refs[: len(weights)]], extra_refs, out_refs[0])

        return call(
            kernel, name + label, out_shape if last else tuple(totals_of),
            (own, *parts, *gains, *weights, *before, *(extras if last else ())),
            scratch if last else (),
            2 * rows * sum(p.shape[0] for p in parts) * depth * sum(widths),
        )

    near = held.shape[0]
    sums = stage("_a", 0, [held], (), False)
    sums = stage("_b", near, brought, sums, False)
    return stage("_c", devices // 2, [far], sums, True)


def project_finish(factor, totals, extra_refs, out_ref):
    cos_ref, sin_ref = extra_refs
    query, key, value = (factor * total for total in totals)
    query_width = query.shape[1]
    key_width = key.shape[1]
    used = query_width + 2 * key_width
    columns = jnp.concatenate(
        [query, key, value, jnp.zeros((query.shape[0], cos_ref.shape[1] - used), jnp.float32)], axis=1
    )
    width = columns.shape[1]
    lane = lax.broadcasted_iota(jnp.int32, columns.shape, 1)
    partner = jnp.where(
        lane % 2 == 1, pltpu.roll(columns, 1, 1), pltpu.roll(columns, width - 1, 1)
    )
    turned = columns * cos_ref[...] + partner * sin_ref[...]
    out_ref[...] = turned.astype(jnp.bfloat16)[:, :used]


def gated_finish(factor, totals, extra_refs, out_ref):
    gate, up = (factor * total for total in totals)
    out_ref[...] = (gate / (1.0 + jnp.exp(-gate)) * up).astype(jnp.bfloat16)


def down_finish(factor, totals, extra_refs, out_ref):
    out_ref[...] = (extra_refs[0][...].astype(jnp.float32) + totals[0]).astype(jnp.bfloat16)


def begin_kernel(device_ref, in_ref, out_ref):
    out_ref[...] = in_ref[...]


def attend_kernel(scale, query_ref, key_ref, value_ref, limit_ref, out_ref):
    heads, rows, head_dim = query_ref.shape
    span = key_ref.shape[0]
    value_heads = key_ref.shape[1] // head_dim
    group = heads // value_heads
    devices = out_ref.shape[0]
    pairs = heads * rows // devices
    place = lax.broadcasted_iota(jnp.int32, (rows, span), 1)
    visible = (place < limit_ref[:, :1])[None]
    for g in range(value_heads):
        lanes = pl.ds(g * head_dim, head_dim)
        queries = query_ref[g * group : (g + 1) * group].reshape(group * rows, head_dim)
        logits = lax.dot_general(
            queries, key_ref[:, lanes], (((1,), (1,)), ((), ())),
            preferred_element_type=jnp.float32,
        ) * scale
        masked = jnp.where(visible, logits.reshape(group, rows, span), MASKED)
        top = jnp.max(masked, axis=2, keepdims=True)
        weights = jnp.where(visible, jnp.exp(masked - top), 0.0)
        total = jnp.sum(weights, axis=2, keepdims=True).reshape(group * rows, 1)
        top = top.reshape(group * rows, 1)
        summed = jnp.dot(
            weights.astype(jnp.bfloat16).reshape(group * rows, span), value_ref[:, lanes],
            preferred_element_type=jnp.float32,
        )
        seen = total > 0.0
        safe = jnp.where(seen, total, 1.0)
        means = (summed / safe).astype(jnp.bfloat16)
        level = jnp.where(seen, top + jnp.log(safe), MASKED)
        across = jnp.transpose(jnp.broadcast_to(level, (group * rows, LANES)))[:8]
        for first in range(0, group * rows, LANES):
            line = across[:, first : first + LANES]
            high = line.astype(jnp.bfloat16)
            rest = line - high.astype(jnp.float32)
            middle = rest.astype(jnp.bfloat16)
            low = (rest - middle.astype(jnp.float32)).astype(jnp.bfloat16)
            row = lax.broadcasted_iota(jnp.int32, line.shape, 0)
            terms = jnp.where(
                row == 0,
                high.astype(jnp.float32),
                jnp.where(row == 1, middle.astype(jnp.float32), low.astype(jnp.float32)),
            ).astype(jnp.bfloat16)
            for begin in range(0, LANES, pairs):
                index = (g * group * rows + first + begin) // pairs
                out_ref[index, :pairs] = means[first + begin : first + begin + pairs]
                out_ref[index, pairs:] = terms


def order_kernel(device_ref, held_ref, out_ref):
    devices = held_ref.shape[0]

    def move(owner, carry):
        place = place_of(lax.bitwise_xor(device_ref[0], owner), devices)
        out_ref[owner] = held_ref[place]
        return carry

    lax.fori_loop(0, devices, move, 0, unroll=4)


def table_kernel(cos_ref, sin_ref, cos_out_ref, sin_out_ref):
    lane = lax.broadcasted_iota(jnp.int32, sin_ref.shape, 1)
    cos_out_ref[...] = cos_ref[...]
    sin_out_ref[...] = jnp.where(lane % 2 == 1, sin_ref[...], -sin_ref[...])


def finish_kernel(numerator_ref, denominator_ref, out_ref):
    out_ref[...] = (numerator_ref[...] / denominator_ref[...]).astype(jnp.bfloat16)


def output_kernel(blocks_ref, weight_ref, residual_ref, mid_ref, total):
    heads, _, head_dim = blocks_ref.shape
    total[...] = jnp.zeros_like(total)

    def step(index, carry):
        block = jnp.concatenate([blocks_ref[2 * index], blocks_ref[2 * index + 1]], axis=1)
        span = pl.ds(pl.multiple_of(index * 2 * head_dim, head_dim), 2 * head_dim)
        total[...] += jnp.dot(block, weight_ref[span, :], preferred_element_type=jnp.float32)
        return carry

    lax.fori_loop(0, heads // 2, step, 0, unroll=4)
    mid_ref[...] = (residual_ref[...].astype(jnp.float32) + total[...]).astype(jnp.bfloat16)


def rotation(first_col, width, positions, head_dim):
    col = jnp.arange(width, dtype=jnp.int32)
    in_head = ((first_col + col - col % 2) % head_dim).astype(jnp.float32)
    frequency = jnp.exp(-(in_head / head_dim) * jnp.log(jnp.float32(ROPE_BASE)))
    angles = positions.astype(jnp.float32)[:, None] * frequency[None, :]
    return jnp.cos(angles), jnp.sin(angles)


def shards(
    hidden_in,
    attn_gain,
    w_query,
    w_key,
    w_value,
    rotated_prefix_keys,
    cache_values,
    w_out,
    ffn_gain,
    w_gate,
    w_up,
    w_down,
    doc_offsets,
    slot_request,
):
    devices = lax.axis_size("ctx")
    device = lax.axis_index("ctx")
    own = lax.optimization_barrier(device.astype(jnp.int32)[None])
    rows, width = hidden_in.shape
    span, value_heads, head_dim = rotated_prefix_keys.shape
    query_width = w_query.shape[1]
    key_width = w_key.shape[1]
    heads = query_width * devices // head_dim
    group = heads // value_heads
    scale = 1.0 / math.sqrt(head_dim)
    slot_index = jnp.arange(rows, dtype=jnp.int32)
    positions = jnp.sum(
        jnp.where(slot_request[:, None] == slot_index[None, :], doc_offsets[None, :], 0), axis=1
    )

    def buffer(*shape, dtype=jnp.bfloat16):
        return jax.ShapeDtypeStruct(shape, dtype)

    def totals(*widths):
        return [pltpu.VMEM((rows, w), jnp.float32) for w in widths]

    used = query_width + 2 * key_width
    padded = -(-used // LANES) * LANES
    query_cos, query_sin = rotation(own * query_width, query_width, positions, head_dim)
    key_cos, key_sin = rotation(own * key_width, key_width, positions, head_dim)
    still = jnp.ones((rows, padded - query_width - key_width), jnp.float32)
    cosine = jnp.concatenate([query_cos, key_cos, still], axis=1)
    sine = jnp.concatenate([query_sin, key_sin, still * 0.0], axis=1)
    table = buffer(rows, padded, dtype=jnp.float32)
    cosine, sine = call(table_kernel, "table", (table, table), (cosine, sine), (), FLOPS["table"])
    begun = call(begin_kernel, "begin", buffer(rows, width), (own, hidden_in))
    sides = (w_key, w_value)
    if width % LANES == 0:
        sides = (w_key.T, w_value.T)
    projected = contract(
        "project", gathered(begun), own, (w_query, *sides), (query_width, key_width, key_width),
        attn_gain, project_finish, (cosine, sine), buffer(rows, used),
    )
    packed = exchange(jnp.broadcast_to(projected[None], (devices, rows, used)))

    def unpacked(first, part_width):
        part = packed[:, :, first : first + part_width]
        if part_width >= head_dim:
            split = part.reshape(devices, rows, part_width // head_dim, head_dim)
            return split.transpose(0, 2, 1, 3).reshape(-1, rows, head_dim)
        run = head_dim // part_width
        return part.reshape(-1, run, rows, part_width).transpose(0, 2, 1, 3).reshape(
            -1, rows, head_dim
        )

    queries = unpacked(0, query_width)
    key_new = unpacked(query_width, key_width)
    value_new = unpacked(query_width + key_width, key_width)
    pairs = heads * rows // devices
    limit = jnp.broadcast_to((positions - own * span)[:, None], (rows, LANES))
    sent = call(
        lambda *refs: attend_kernel(scale, *refs), "attend", buffer(devices, pairs + 8, LANES),
        (
            queries,
            rotated_prefix_keys.reshape(span, value_heads * head_dim),
            cache_values.reshape(span, value_heads * head_dim),
            limit,
        ),
        (),
        4 * heads * rows * span * head_dim,
    )
    got = exchange(sent)
    first_pair = device * pairs
    means = got[:, :pairs].astype(jnp.float32)
    terms = lax.dynamic_slice_in_dim(
        got[:, pairs : pairs + 3].astype(jnp.float32), first_pair % LANES, pairs, 2
    )
    levels = terms[:, 0] + terms[:, 1] + terms[:, 2]

    def mine(every):
        return lax.dynamic_slice_in_dim(
            every.reshape(heads * rows, head_dim), first_pair, pairs, 0
        ).astype(jnp.float32)

    def spread(new):
        return jnp.broadcast_to(new[:, None], (value_heads, group, rows, head_dim))

    own_score = jnp.sum(mine(queries) * mine(spread(key_new)), axis=1) * scale
    own_value = mine(spread(value_new))
    peak = jnp.maximum(jnp.max(levels, axis=0), own_score)
    shares = jnp.exp(levels - peak[None, :])
    own_share = jnp.exp(own_score - peak)
    numerator = jnp.sum(shares[..., None] * means, axis=0) + own_share[:, None] * own_value
    denominator = jnp.sum(shares, axis=0) + own_share
    attn_part = call(
        finish_kernel, "finish", buffer(pairs, head_dim), (numerator, denominator[:, None]), (),
        FLOPS["finish"],
    )
    held = together(gathered(attn_part))
    attn_all = call(
        order_kernel, "order", buffer(devices, pairs, head_dim), (own, held)
    )
    mid_part = call(
        output_kernel, "output", buffer(rows, width),
        (attn_all.reshape(heads, rows, head_dim), w_out, hidden_in),
        totals(width),
        2 * rows * heads * head_dim * width,
    )
    hidden_width = w_gate.shape[1]
    hidden = contract(
        "gated", gathered(mid_part), own, (w_gate, w_up), (hidden_width, hidden_width),
        ffn_gain, gated_finish, (), buffer(rows, hidden_width),
    )
    hidden = call(begin_kernel, "relay", buffer(rows, hidden_width), (own, hidden))
    return contract(
        "down", gathered(hidden), own, (w_down,), (width,),
        None, down_finish, (mid_part,), buffer(rows, width),
    )


def solution(mesh):
    return jax.shard_map(
        shards,
        mesh=mesh,
        in_specs=(
            P("groups", "ctx"),
            P(),
            P(None, "ctx"),
            P(None, "ctx"),
            P(None, "ctx"),
            P(("groups", "ctx"), None, None),
            P(("groups", "ctx"), None, None),
            P(None, "ctx"),
            P(),
            P(None, "ctx"),
            P(None, "ctx"),
            P(None, "ctx"),
            P("groups"),
            P("groups"),
        ),
        out_specs=P("groups", "ctx"),
        check_vma=False,
    )
```

```python
import math

import jax
import jax.numpy as jnp
from jax import lax
from jax.experimental import pallas as pl
from jax.experimental.pallas import tpu as pltpu
from jax.sharding import PartitionSpec as P


NORM_EPSILON = 1e-05
ROPE_BASE = 500000.0
MASKED = -1e30


LANES = 128
FLOPS = {"begin": 10**11, "table": 10**11, "finish": 10**11, "output": 10**11, "relay": 10**11, "merge_next": 10**11, "output_a": 10**11}
VMEM = pl.BlockSpec(memory_space=pltpu.VMEM)
SMEM = pl.BlockSpec(memory_space=pltpu.SMEM)


def exchange(blocks):
    return lax.all_to_all(blocks, "ctx", 0, 0)


def digits(devices):
    rest, stride, place, out = devices // 2, devices, 1, []
    while rest > 1:
        radix = 4 if rest % 4 == 0 else 2
        stride //= radix
        out.append((stride, radix, place))
        place *= radix
        rest //= radix
    return out + [(1, 2, place)]


def mask_at(place_index, devices):
    return sum(((place_index // place) % radix) * stride for stride, radix, place in digits(devices))


def place_of(mask, devices):
    return sum(((mask // stride) % radix) * place for stride, radix, place in digits(devices))


def shifted(part, mask):
    devices = lax.axis_size("ctx")
    return lax.ppermute(part, "ctx", [(index, index ^ mask) for index in range(devices)])


def gathered(part):
    devices = lax.axis_size("ctx")
    held = part[None]
    *rounds, last, _ = digits(devices)

    def arrive(stride, radix):
        return [shifted(held, stride * digit) for digit in range(1, radix)]

    for stride, radix, _ in rounds:
        arrived = arrive(stride, radix)
        held = jnp.concatenate([held] + arrived, axis=0)
    brought = arrive(*last[:2])
    near = jnp.concatenate([held] + brought, axis=0)
    return held, brought, shifted(near, 1)


def together(pieces):
    held, brought, far = pieces
    return jnp.concatenate([held, *brought, far], axis=0)


def call(body, name, out_shape, args, scratch=(), flops=0):
    moved = sum(a.size * a.dtype.itemsize for a in args)
    return pl.pallas_call(
        body,
        out_shape=out_shape,
        in_specs=[SMEM if a.dtype == jnp.int32 and a.ndim == 1 else VMEM for a in args],
        out_specs=jax.tree.map(lambda _: VMEM, out_shape),
        scratch_shapes=list(scratch),
        compiler_params=pltpu.CompilerParams(vmem_limit_bytes=6 << 20),
        cost_estimate=pl.CostEstimate(flops=FLOPS.get(name, flops), bytes_accessed=moved, transcendentals=0),
    )(*args)


def accumulate(device_ref, devices, pieces, owner_of, gain_ref, weight_refs, total_refs, square_ref):
    for first, piece_ref in pieces:
        places, _, depth = piece_ref.shape

        def step(index, carry):
            owner = owner_of(device_ref[0], first + index, devices)
            block = piece_ref[index]
            if gain_ref is not None:
                wide = block.astype(jnp.float32)
                block = (wide * gain_ref[owner]).astype(jnp.bfloat16)
                square_ref[...] += sum(
                    wide[:, lane : lane + LANES] * wide[:, lane : lane + LANES]
                    for lane in range(0, depth, LANES)
                ) if depth % LANES == 0 else jnp.broadcast_to(
                    jnp.sum(wide * wide, axis=1, keepdims=True) / LANES, square_ref.shape
                )
            span = pl.ds(pl.multiple_of(owner * depth, depth), depth)
            for weight_ref, total_ref in zip(weight_refs, total_refs):
                if weight_ref.shape[1] == devices * depth:
                    total_ref[...] += lax.dot_general(
                        block, weight_ref[:, span], (((1,), (1,)), ((), ())),
                        preferred_element_type=jnp.float32,
                    )
                else:
                    total_ref[...] += jnp.dot(
                        block, weight_ref[span, :], preferred_element_type=jnp.float32
                    )
            return carry

        lax.fori_loop(0, places, step, 0, unroll=4)


def by_place(device, place_index, devices):
    return lax.bitwise_xor(device, mask_at(place_index, devices))


def contract(name, pieces, own, weights, widths, gain, finish, extras, out_shape, owner_of=by_place):
    held, brought, far = pieces
    devices = lax.axis_size("ctx")
    _, rows, depth = held.shape
    normed = gain is not None
    gains = [gain.reshape(devices, 1, depth)] if normed else []
    totals_of = [jax.ShapeDtypeStruct((rows, w), jnp.float32) for w in widths]
    if normed:
        totals_of.append(jax.ShapeDtypeStruct((rows, LANES), jnp.float32))
    scratch = [pltpu.VMEM(t.shape, t.dtype) for t in totals_of]

    def stage(label, first, parts, before, last):
        def kernel(device_ref, *refs):
            refs = list(refs)
            take = lambda count: [refs.pop(0) for _ in range(count)]
            part_refs, gain_refs, weight_refs = take(len(parts)), take(len(gains)), take(len(weights))
            before_refs = take(len(before))
            extra_refs = take(len(extras)) if last else []
            out_refs = take(1 if last else 0)
            total_refs = refs
            for index, total_ref in enumerate(total_refs):
                if before:
                    total_ref[...] = before_refs[index][...]
                else:
                    total_ref[...] = jnp.zeros_like(total_ref)
            place, placed = first, []
            for part_ref in part_refs:
                placed.append((place, part_ref))
                place += part_ref.shape[0]
            accumulate(
                device_ref, devices, placed, owner_of, gain_refs[0] if normed else None,
                weight_refs, total_refs[: len(weights)], total_refs[-1],
            )
            if last:
                factor = None
                if normed:
                    mean = jnp.sum(total_refs[-1][...], axis=1, keepdims=True) / (devices * depth)
                    factor = lax.rsqrt(mean + NORM_EPSILON)
                finish(factor, [t[...] for t in total_refs[: len(weights)]], extra_refs, out_refs[0])

        return call(
            kernel, name + label, out_shape if last else tuple(totals_of),
            (own, *parts, *gains, *weights, *before, *(extras if last else ())),
            scratch if last else (),
            2 * rows * sum(p.shape[0] for p in parts) * depth * sum(widths),
        )

    near = held.shape[0]
    sums = stage("_a", 0, [held], (), False)
    sums = stage("_b", near, brought, sums, False)
    return stage("_c", devices // 2, [far], sums, True)


def project_finish(factor, totals, extra_refs, out_ref):
    cos_ref, sin_ref = extra_refs
    query, key, value = (factor * total for total in totals)
    query_width = query.shape[1]
    key_width = key.shape[1]
    used = query_width + 2 * key_width
    columns = jnp.concatenate(
        [query, key, value, jnp.zeros((query.shape[0], cos_ref.shape[1] - used), jnp.float32)], axis=1
    )
    width = columns.shape[1]
    lane = lax.broadcasted_iota(jnp.int32, columns.shape, 1)
    partner = jnp.where(
        lane % 2 == 1, pltpu.roll(columns, 1, 1), pltpu.roll(columns, width - 1, 1)
    )
    turned = columns * cos_ref[...] + partner * sin_ref[...]
    out_ref[...] = turned.astype(jnp.bfloat16)[:, :used]


def gated_finish(factor, totals, extra_refs, out_ref):
    gate, up = (factor * total for total in totals)
    out_ref[...] = (gate / (1.0 + jnp.exp(-gate)) * up).astype(jnp.bfloat16)


def down_finish(factor, totals, extra_refs, out_ref):
    out_ref[...] = (extra_refs[0][...].astype(jnp.float32) + totals[0]).astype(jnp.bfloat16)


def begin_kernel(device_ref, in_ref, out_ref):
    out_ref[...] = in_ref[...]


def attend_kernel(scale, query_ref, key_ref, value_ref, limit_ref, out_ref):
    heads, rows, head_dim = query_ref.shape
    span = key_ref.shape[0]
    value_heads = key_ref.shape[1] // head_dim
    group = heads // value_heads
    devices = out_ref.shape[0]
    pairs = heads * rows // devices
    place = lax.broadcasted_iota(jnp.int32, (rows, span), 1)
    visible = (place < limit_ref[:, :1])[None]
    for g in range(value_heads):
        lanes = pl.ds(g * head_dim, head_dim)
        queries = query_ref[g * group : (g + 1) * group].reshape(group * rows, head_dim)
        logits = lax.dot_general(
            queries, key_ref[:, lanes], (((1,), (1,)), ((), ())),
            preferred_element_type=jnp.float32,
        ) * scale
        masked = jnp.where(visible, logits.reshape(group, rows, span), MASKED)
        top = jnp.max(masked, axis=2, keepdims=True)
        weights = jnp.where(visible, jnp.exp(masked - top), 0.0)
        total = jnp.sum(weights, axis=2, keepdims=True).reshape(group * rows, 1)
        top = top.reshape(group * rows, 1)
        summed = jnp.dot(
            weights.astype(jnp.bfloat16).reshape(group * rows, span), value_ref[:, lanes],
            preferred_element_type=jnp.float32,
        )
        seen = total > 0.0
        safe = jnp.where(seen, total, 1.0)
        means = (summed / safe).astype(jnp.bfloat16)
        level = jnp.where(seen, top + jnp.log(safe), MASKED)
        across = jnp.transpose(jnp.broadcast_to(level, (group * rows, LANES)))[:8]
        for first in range(0, group * rows, LANES):
            line = across[:, first : first + LANES]
            high = line.astype(jnp.bfloat16)
            rest = line - high.astype(jnp.float32)
            middle = rest.astype(jnp.bfloat16)
            low = (rest - middle.astype(jnp.float32)).astype(jnp.bfloat16)
            row = lax.broadcasted_iota(jnp.int32, line.shape, 0)
            terms = jnp.where(
                row == 0,
                high.astype(jnp.float32),
                jnp.where(row == 1, middle.astype(jnp.float32), low.astype(jnp.float32)),
            ).astype(jnp.bfloat16)
            for begin in range(0, LANES, pairs):
                index = (g * group * rows + first + begin) // pairs
                out_ref[index, :pairs] = means[first + begin : first + begin + pairs]
                out_ref[index, pairs:] = terms


def terms_of(level):
    line = jnp.transpose(level)[:8]
    high = line.astype(jnp.bfloat16).astype(jnp.float32)
    rest = line - high
    middle = rest.astype(jnp.bfloat16).astype(jnp.float32)
    row = lax.broadcasted_iota(jnp.int32, line.shape, 0)
    return jnp.where(row == 0, high, jnp.where(row == 1, middle, rest - middle)).astype(jnp.bfloat16)


def read_message(message):
    pairs = message.shape[0] - 8
    terms = message[pairs:].astype(jnp.float32)
    line = terms[0:1] + terms[1:2] + terms[2:3]
    return message[:pairs].astype(jnp.float32), jnp.transpose(jnp.broadcast_to(line, (LANES, LANES)))


def merge(parts):
    peak = parts[0][1]
    for _, level in parts[1:]:
        peak = jnp.maximum(peak, level)
    shares = [jnp.exp(level - peak) for _, level in parts]
    denominator = sum(shares[1:], shares[0])
    numerator = shares[0] * parts[0][0]
    for share, (mean, _) in zip(shares[1:], parts[1:]):
        numerator = numerator + share * mean
    return numerator / denominator, peak + jnp.log(denominator)


def put_message(message_ref, mean, level):
    pairs = mean.shape[0]
    message_ref[:pairs] = mean.astype(jnp.bfloat16)
    message_ref[pairs:] = terms_of(level)


def half_kernel(scale, head_dim, sends, device_ref, blocks_ref, key_ref, value_ref, limit_ref, *out_refs):
    places, rows, _ = blocks_ref.shape
    span = key_ref.shape[0]
    value_heads = key_ref.shape[1] // head_dim
    units = places // value_heads
    local = LANES // (value_heads * rows)
    count = units * local
    group_index = lax.div(device_ref[0], 2 * units)
    visible = (lax.broadcasted_iota(jnp.int32, (rows, span), 1) < limit_ref[:, :1])[None]
    means = [[] for _ in range(units)]
    levels = [[] for _ in range(units)]
    for g in range(value_heads):
        lanes = pl.ds(g * head_dim, head_dim)
        parts = []
        for unit in range(units):
            block = blocks_ref[unit * value_heads + lax.bitwise_xor(group_index, g)]
            parts += [block[:, h * head_dim : (h + 1) * head_dim] for h in range(local)]
        logits = lax.dot_general(
            jnp.concatenate(parts, axis=0), key_ref[:, lanes], (((1,), (1,)), ((), ())),
            preferred_element_type=jnp.float32,
        ) * scale
        masked = jnp.where(visible, logits.reshape(count, rows, span), MASKED)
        top = jnp.max(masked, axis=2, keepdims=True)
        weights = jnp.where(visible, jnp.exp(masked - top), 0.0)
        total = jnp.sum(weights, axis=2, keepdims=True).reshape(count * rows, 1)
        top = top.reshape(count * rows, 1)
        summed = jnp.dot(
            weights.astype(jnp.bfloat16).reshape(count * rows, span), value_ref[:, lanes],
            preferred_element_type=jnp.float32,
        )
        seen = total > 0.0
        safe = jnp.where(seen, total, 1.0)
        mean = summed / safe
        level = jnp.broadcast_to(jnp.where(seen, top + jnp.log(safe), MASKED), (count * rows, LANES))
        run = local * rows
        for unit in range(units):
            means[unit].append(mean[unit * run : (unit + 1) * run])
            levels[unit].append(level[unit * run : (unit + 1) * run])
    for unit in range(units):
        mean = jnp.concatenate(means[unit], axis=0)
        level = jnp.concatenate(levels[unit], axis=0)
        if sends:
            put_message(out_refs[0].at[unit], mean, level)
        else:
            out_refs[0][unit] = mean
            out_refs[1][unit] = level


def merge_core_kernel(mean_ref, level_ref, message_ref, sent_ref, mean_out_ref, level_out_ref):
    for unit in (1, 0):
        mean, level = merge([(mean_ref[unit], level_ref[unit]), read_message(message_ref[unit])])
        if unit == 1:
            put_message(sent_ref, mean, level)
        else:
            mean_out_ref[...] = mean
            level_out_ref[...] = level


def merge_next_kernel(mean_ref, level_ref, message_ref, sent_ref, mean_out_ref, level_out_ref):
    mean, level = merge([(mean_ref[...], level_ref[...]), read_message(message_ref[...])])
    put_message(sent_ref, mean, level)
    mean_out_ref[...] = mean
    level_out_ref[...] = level


def fresh_kernel(scale, head_dim, value_heads, key_width, device_ref, near_ref, far_ref, score_ref, value_ref):
    _, rows, used = far_ref.shape
    query_width = used - 2 * key_width
    run = head_dim // key_width
    units = run // 2
    group_index = lax.div(device_ref[0], run)
    core = lax.rem(device_ref[0], 2)
    step = lax.rem(lax.div(device_ref[0], 2), units)
    for g in range(value_heads):
        turned = lax.bitwise_xor(group_index, g)
        news = []
        for index in range(run):
            place = lax.bitwise_xor(step, index // 2) * value_heads + turned
            block = jnp.where(core == index % 2, near_ref[place], far_ref[place])
            news.append(block[:, query_width:])
        key = jnp.concatenate([new[:, :key_width] for new in news], axis=1).astype(jnp.float32)
        value = jnp.concatenate([new[:, key_width:] for new in news], axis=1).astype(jnp.float32)
        queries = far_ref[turned]
        for h in range(query_width // head_dim):
            query = queries[:, h * head_dim : (h + 1) * head_dim].astype(jnp.float32)
            score = jnp.sum(query * key, axis=1, keepdims=True) * scale
            span = pl.ds((g * (query_width // head_dim) + h) * rows, rows)
            score_ref[span, :] = jnp.broadcast_to(score, (rows, LANES))
            value_ref[span, :] = value


def settle_kernel(
    rows, mean_ref, level_ref, *refs
):
    *message_refs, score_ref, value_ref, out_ref = refs
    parts = [(mean_ref[...], level_ref[...])]
    parts += [read_message(message_ref[...]) for message_ref in message_refs]
    parts.append((value_ref[...], score_ref[...]))
    mean, _ = merge(parts)
    done = mean.astype(jnp.bfloat16)
    owners, _, width = out_ref.shape
    local = width // LANES
    for g in range(owners):
        first = g * local * rows
        out_ref[g] = jnp.concatenate(
            [done[first + h * rows : first + (h + 1) * rows] for h in range(local)], axis=1
        )


def residual_finish(factor, totals, extra_refs, out_ref):
    out_ref[...] = (extra_refs[0][...].astype(jnp.float32) + totals[0]).astype(jnp.bfloat16)


def by_group(device, place_index, devices):
    (stride, groups, _), (step, _, _), _ = digits(devices)
    place_in_group = lax.bitwise_xor(lax.rem(device, stride), 1)
    far = lax.div(place_index, devices // 2) if not isinstance(place_index, int) else place_index // (devices // 2)
    near_place = lax.rem(place_index, devices // 2)
    turned = lax.bitwise_xor(place_in_group, lax.div(near_place, groups) * step)
    return lax.rem(near_place, groups) * stride + lax.bitwise_xor(turned, far)


def order_kernel(device_ref, held_ref, out_ref):
    devices = held_ref.shape[0]

    def move(owner, carry):
        place = place_of(lax.bitwise_xor(device_ref[0], owner), devices)
        out_ref[owner] = held_ref[place]
        return carry

    lax.fori_loop(0, devices, move, 0, unroll=4)


def table_kernel(cos_ref, sin_ref, cos_out_ref, sin_out_ref):
    lane = lax.broadcasted_iota(jnp.int32, sin_ref.shape, 1)
    cos_out_ref[...] = cos_ref[...]
    sin_out_ref[...] = jnp.where(lane % 2 == 1, sin_ref[...], -sin_ref[...])


def finish_kernel(numerator_ref, denominator_ref, out_ref):
    out_ref[...] = (numerator_ref[...] / denominator_ref[...]).astype(jnp.bfloat16)


def output_kernel(blocks_ref, weight_ref, residual_ref, mid_ref, total):
    heads, _, head_dim = blocks_ref.shape
    total[...] = jnp.zeros_like(total)

    def step(index, carry):
        block = jnp.concatenate([blocks_ref[2 * index], blocks_ref[2 * index + 1]], axis=1)
        span = pl.ds(pl.multiple_of(index * 2 * head_dim, head_dim), 2 * head_dim)
        total[...] += jnp.dot(block, weight_ref[span, :], preferred_element_type=jnp.float32)
        return carry

    lax.fori_loop(0, heads // 2, step, 0, unroll=4)
    mid_ref[...] = (residual_ref[...].astype(jnp.float32) + total[...]).astype(jnp.bfloat16)


def rotation(first_col, width, positions, head_dim):
    col = jnp.arange(width, dtype=jnp.int32)
    in_head = ((first_col + col - col % 2) % head_dim).astype(jnp.float32)
    frequency = jnp.exp(-(in_head / head_dim) * jnp.log(jnp.float32(ROPE_BASE)))
    angles = positions.astype(jnp.float32)[:, None] * frequency[None, :]
    return jnp.cos(angles), jnp.sin(angles)


def shards(
    hidden_in,
    attn_gain,
    w_query,
    w_key,
    w_value,
    rotated_prefix_keys,
    cache_values,
    w_out,
    ffn_gain,
    w_gate,
    w_up,
    w_down,
    doc_offsets,
    slot_request,
):
    devices = lax.axis_size("ctx")
    device = lax.axis_index("ctx")
    own = lax.optimization_barrier(device.astype(jnp.int32)[None])
    rows, width = hidden_in.shape
    span, value_heads, head_dim = rotated_prefix_keys.shape
    query_width = w_query.shape[1]
    key_width = w_key.shape[1]
    heads = query_width * devices // head_dim
    group = heads // value_heads
    scale = 1.0 / math.sqrt(head_dim)
    slot_index = jnp.arange(rows, dtype=jnp.int32)
    positions = jnp.sum(
        jnp.where(slot_request[:, None] == slot_index[None, :], doc_offsets[None, :], 0), axis=1
    )

    def buffer(*shape, dtype=jnp.bfloat16):
        return jax.ShapeDtypeStruct(shape, dtype)

    def totals(*widths):
        return [pltpu.VMEM((rows, w), jnp.float32) for w in widths]

    used = query_width + 2 * key_width
    padded = -(-used // LANES) * LANES
    query_cos, query_sin = rotation(own * query_width, query_width, positions, head_dim)
    key_cos, key_sin = rotation(own * key_width, key_width, positions, head_dim)
    still = jnp.ones((rows, padded - query_width - key_width), jnp.float32)
    cosine = jnp.concatenate([query_cos, key_cos, still], axis=1)
    sine = jnp.concatenate([query_sin, key_sin, still * 0.0], axis=1)
    table = buffer(rows, padded, dtype=jnp.float32)
    cosine, sine = call(table_kernel, "table", (table, table), (cosine, sine), (), FLOPS["table"])
    begun = call(begin_kernel, "begin", buffer(rows, width), (own, hidden_in))
    sides = (w_key, w_value)
    if width % LANES == 0:
        sides = (w_key.T, w_value.T)
    projected = contract(
        "project", gathered(begun), own, (w_query, *sides), (query_width, key_width, key_width),
        attn_gain, project_finish, (cosine, sine), buffer(rows, used),
    )
    limit = jnp.broadcast_to((positions - own * span)[:, None], (rows, LANES))
    keys = rotated_prefix_keys.reshape(span, value_heads * head_dim)
    values = cache_values.reshape(span, value_heads * head_dim)
    rounds = digits(devices)
    if (
        len(rounds) == 3
        and rounds[0][1] == value_heads
        and rounds[1][1] == 2
        and head_dim == LANES
        and value_heads * (query_width // head_dim) * rows == LANES
    ):
        held, brought, far = gathered(projected)
        near = jnp.concatenate([held] + brought, axis=0)
        unit = (LANES, LANES)
        message = buffer(LANES + 8, LANES)
        wide = buffer(*unit, dtype=jnp.float32)
        pair = buffer(2, *unit, dtype=jnp.float32)
        work = 2 * heads * rows * span * head_dim

        def half(name, blocks, sends, out_shape):
            return call(
                lambda *refs: half_kernel(scale, head_dim, sends, *refs), name, out_shape,
                (own, blocks, keys, values, limit), (), work,
            )

        given = half("attend_near", near, True, buffer(2, LANES + 8, LANES))
        taken = shifted(given, 1)
        mean, level = half("attend_far", far, False, (pair, pair))
        given, mean, level = call(
            merge_core_kernel, "merge_core", (message, wide, wide), (mean, level, taken)
        )
        taken = shifted(given, rounds[1][0])
        given, mean, level = call(
            merge_next_kernel, "merge_next", (message, wide, wide), (mean, level, taken)
        )
        taken = [shifted(given, rounds[0][0] * digit) for digit in range(1, rounds[0][1])]
        score, value = call(
            lambda *refs: fresh_kernel(scale, head_dim, value_heads, key_width, *refs), "fresh",
            (wide, wide), (own, near, far),
        )
        done = call(
            lambda *refs: settle_kernel(rows, *refs), "settle",
            buffer(value_heads, rows, query_width), (mean, level, *taken, score, value),
        )
        brought = [shifted(done, rounds[1][0])]
        far = shifted(jnp.concatenate([done] + brought, axis=0), 1)
        mid_part = contract(
            "output", (done, brought, far), own, (w_out,), (width,),
            None, residual_finish, (hidden_in,), buffer(rows, width), by_group,
        )
    else:
        packed = exchange(jnp.broadcast_to(projected[None], (devices, rows, used)))

        def unpacked(first, part_width):
            part = packed[:, :, first : first + part_width]
            if part_width >= head_dim:
                split = part.reshape(devices, rows, part_width // head_dim, head_dim)
                return split.transpose(0, 2, 1, 3).reshape(-1, rows, head_dim)
            run = head_dim // part_width
            return part.reshape(-1, run, rows, part_width).transpose(0, 2, 1, 3).reshape(
                -1, rows, head_dim
            )

        queries = unpacked(0, query_width)
        key_new = unpacked(query_width, key_width)
        value_new = unpacked(query_width + key_width, key_width)
        pairs = heads * rows // devices
        sent = call(
            lambda *refs: attend_kernel(scale, *refs), "attend", buffer(devices, pairs + 8, LANES),
            (
                queries,
                keys,
                values,
                limit,
            ),
            (),
            4 * heads * rows * span * head_dim,
        )
        got = exchange(sent)
        first_pair = device * pairs
        means = got[:, :pairs].astype(jnp.float32)
        terms = lax.dynamic_slice_in_dim(
            got[:, pairs : pairs + 3].astype(jnp.float32), first_pair % LANES, pairs, 2
        )
        levels = terms[:, 0] + terms[:, 1] + terms[:, 2]

        def mine(every):
            return lax.dynamic_slice_in_dim(
                every.reshape(heads * rows, head_dim), first_pair, pairs, 0
            ).astype(jnp.float32)

        def spread(new):
            return jnp.broadcast_to(new[:, None], (value_heads, group, rows, head_dim))

        own_score = jnp.sum(mine(queries) * mine(spread(key_new)), axis=1) * scale
        own_value = mine(spread(value_new))
        peak = jnp.maximum(jnp.max(levels, axis=0), own_score)
        shares = jnp.exp(levels - peak[None, :])
        own_share = jnp.exp(own_score - peak)
        numerator = jnp.sum(shares[..., None] * means, axis=0) + own_share[:, None] * own_value
        denominator = jnp.sum(shares, axis=0) + own_share
        attn_part = call(
            finish_kernel, "finish", buffer(pairs, head_dim), (numerator, denominator[:, None]), (),
            FLOPS["finish"],
        )
        held = together(gathered(attn_part))
        attn_all = call(
            order_kernel, "order", buffer(devices, pairs, head_dim), (own, held)
        )
        mid_part = call(
            output_kernel, "output", buffer(rows, width),
            (attn_all.reshape(heads, rows, head_dim), w_out, hidden_in),
            totals(width),
            2 * rows * heads * head_dim * width,
        )
    hidden_width = w_gate.shape[1]
    hidden = contract(
        "gated", gathered(mid_part), own, (w_gate, w_up), (hidden_width, hidden_width),
        ffn_gain, gated_finish, (), buffer(rows, hidden_width),
    )
    hidden = call(begin_kernel, "relay", buffer(rows, hidden_width), (own, hidden))
    return contract(
        "down", gathered(hidden), own, (w_down,), (width,),
        None, down_finish, (mid_part,), buffer(rows, width),
    )


def solution(mesh):
    return jax.shard_map(
        shards,
        mesh=mesh,
        in_specs=(
            P("groups", "ctx"),
            P(),
            P(None, "ctx"),
            P(None, "ctx"),
            P(None, "ctx"),
            P(("groups", "ctx"), None, None),
            P(("groups", "ctx"), None, None),
            P(None, "ctx"),
            P(),
            P(None, "ctx"),
            P(None, "ctx"),
            P(None, "ctx"),
            P("groups"),
            P("groups"),
        ),
        out_specs=P("groups", "ctx"),
        check_vma=False,
    )
```

```python
import math

import jax
import jax.numpy as jnp
from jax import lax
from jax.experimental import pallas as pl
from jax.experimental.pallas import tpu as pltpu
from jax.sharding import PartitionSpec as P


NORM_EPSILON = 1e-05
ROPE_BASE = 500000.0
MASKED = -1e30


LANES = 128
FLOPS = {"begin": 10**11, "table": 10**11, "finish": 10**11, "output": 10**11, "relay": 10**11, "merge_next": 10**11, "output_a": 10**11}
VMEM = pl.BlockSpec(memory_space=pltpu.VMEM)
SMEM = pl.BlockSpec(memory_space=pltpu.SMEM)


def exchange(blocks):
    return lax.all_to_all(blocks, "ctx", 0, 0)


def digits(devices):
    rest, stride, place, out = devices // 2, devices, 1, []
    while rest > 1:
        radix = 4 if rest % 4 == 0 else 2
        stride //= radix
        out.append((stride, radix, place))
        place *= radix
        rest //= radix
    return out + [(1, 2, place)]


def mask_at(place_index, devices):
    return sum(((place_index // place) % radix) * stride for stride, radix, place in digits(devices))


def place_of(mask, devices):
    return sum(((mask // stride) % radix) * place for stride, radix, place in digits(devices))


def shifted(part, mask):
    devices = lax.axis_size("ctx")
    return lax.ppermute(part, "ctx", [(index, index ^ mask) for index in range(devices)])


def gathered(part, given=None):
    devices = lax.axis_size("ctx")
    held = part[None]
    *rounds, last, _ = digits(devices)

    def arrive(stride, radix, held):
        return [shifted(held, stride * digit) for digit in range(1, radix)]

    for stride, radix, _ in rounds:
        arrived = arrive(stride, radix, held if given is None else given[None])
        given = None
        held = jnp.concatenate([held] + arrived, axis=0)
    return pieces_of(held, *last[:2])


def pieces_of(held, stride, radix):
    brought = [shifted(held, stride * digit) for digit in range(1, radix)]
    brought = brought[0] if radix == 2 else jnp.concatenate(brought, axis=0)
    far = shifted(held, 1)
    return held, far, brought, shifted(brought, 1)


def together(pieces):
    held, far, brought, far_brought = pieces
    return jnp.concatenate([held, brought, far, far_brought], axis=0)


def call(body, name, out_shape, args, scratch=(), flops=0):
    moved = sum(a.size * a.dtype.itemsize for a in args)
    return pl.pallas_call(
        body,
        out_shape=out_shape,
        in_specs=[SMEM if a.dtype == jnp.int32 and a.ndim == 1 else VMEM for a in args],
        out_specs=jax.tree.map(lambda _: VMEM, out_shape),
        scratch_shapes=list(scratch),
        compiler_params=pltpu.CompilerParams(vmem_limit_bytes=6 << 20),
        cost_estimate=pl.CostEstimate(flops=FLOPS.get(name, flops), bytes_accessed=moved, transcendentals=0),
    )(*args)


def accumulate(device_ref, devices, pieces, owner_of, gain_ref, weight_refs, total_refs, square_ref):
    for first, piece_ref in pieces:
        places, _, depth = piece_ref.shape

        def step(index, carry):
            owner = owner_of(device_ref[0], first + index, devices)
            block = piece_ref[index]
            if gain_ref is not None:
                wide = block.astype(jnp.float32)
                block = (wide * gain_ref[owner]).astype(jnp.bfloat16)
                square_ref[...] += sum(
                    wide[:, lane : lane + LANES] * wide[:, lane : lane + LANES]
                    for lane in range(0, depth, LANES)
                ) if depth % LANES == 0 else jnp.broadcast_to(
                    jnp.sum(wide * wide, axis=1, keepdims=True) / LANES, square_ref.shape
                )
            span = pl.ds(pl.multiple_of(owner * depth, depth), depth)
            for weight_ref, total_ref in zip(weight_refs, total_refs):
                if weight_ref.shape[1] == devices * depth:
                    total_ref[...] += lax.dot_general(
                        block, weight_ref[:, span], (((1,), (1,)), ((), ())),
                        preferred_element_type=jnp.float32,
                    )
                else:
                    total_ref[...] += jnp.dot(
                        block, weight_ref[span, :], preferred_element_type=jnp.float32
                    )
            return carry

        lax.fori_loop(0, places, step, 0, unroll=4)


def by_place(device, place_index, devices):
    return lax.bitwise_xor(device, mask_at(place_index, devices))


def contract(name, pieces, own, weights, widths, gain, finish, extras, out_shape, owner_of=by_place):
    devices = lax.axis_size("ctx")
    near, rows, depth = pieces[0].shape
    normed = gain is not None
    gains = [gain.reshape(devices, 1, depth)] if normed else []
    totals_of = [jax.ShapeDtypeStruct((rows, w), jnp.float32) for w in widths]
    if normed:
        totals_of.append(jax.ShapeDtypeStruct((rows, LANES), jnp.float32))
    scratch = [pltpu.VMEM(t.shape, t.dtype) for t in totals_of]

    def stage(label, first, parts, before, last):
        def kernel(device_ref, *refs):
            refs = list(refs)
            take = lambda count: [refs.pop(0) for _ in range(count)]
            part_refs, gain_refs, weight_refs = take(len(parts)), take(len(gains)), take(len(weights))
            before_refs = take(len(before))
            extra_refs = take(len(extras)) if last else []
            out_refs = take(1 if last else 0)
            total_refs = refs
            for index, total_ref in enumerate(total_refs):
                if before:
                    total_ref[...] = before_refs[index][...]
                else:
                    total_ref[...] = jnp.zeros_like(total_ref)
            place, placed = first, []
            for part_ref in part_refs:
                placed.append((place, part_ref))
                place += part_ref.shape[0]
            accumulate(
                device_ref, devices, placed, owner_of, gain_refs[0] if normed else None,
                weight_refs, total_refs[: len(weights)], total_refs[-1],
            )
            if last:
                factor = None
                if normed:
                    mean = jnp.sum(total_refs[-1][...], axis=1, keepdims=True) / (devices * depth)
                    factor = lax.rsqrt(mean + NORM_EPSILON)
                finish(factor, [t[...] for t in total_refs[: len(weights)]], extra_refs, out_refs[0])

        return call(
            kernel, name + label, out_shape if last else tuple(totals_of),
            (own, *parts, *gains, *weights, *before, *(extras if last else ())),
            scratch if last else (),
            2 * rows * sum(p.shape[0] for p in parts) * depth * sum(widths),
        )

    sums = ()
    firsts = (0, devices // 2, near, devices // 2 + near)
    for label, first, piece in zip(("_a", "_b", "_c", "_d"), firsts, pieces):
        sums = stage(label, first, [piece], sums, label == "_d")
    return sums


def project_finish(factor, totals, extra_refs, out_ref):
    cos_ref, sin_ref = extra_refs
    query, key, value = (factor * total for total in totals)
    query_width = query.shape[1]
    key_width = key.shape[1]
    used = query_width + 2 * key_width
    columns = jnp.concatenate(
        [query, key, value, jnp.zeros((query.shape[0], cos_ref.shape[1] - used), jnp.float32)], axis=1
    )
    width = columns.shape[1]
    lane = lax.broadcasted_iota(jnp.int32, columns.shape, 1)
    partner = jnp.where(
        lane % 2 == 1, pltpu.roll(columns, 1, 1), pltpu.roll(columns, width - 1, 1)
    )
    turned = columns * cos_ref[...] + partner * sin_ref[...]
    out_ref[...] = turned.astype(jnp.bfloat16)[:, :used]


def gated_finish(factor, totals, extra_refs, out_ref):
    gate, up = (factor * total for total in totals)
    out_ref[...] = (gate / (1.0 + jnp.exp(-gate)) * up).astype(jnp.bfloat16)


def down_finish(factor, totals, extra_refs, out_ref):
    out_ref[...] = (extra_refs[0][...].astype(jnp.float32) + totals[0]).astype(jnp.bfloat16)


def begin_kernel(device_ref, in_ref, out_ref):
    out_ref[...] = in_ref[...]


def attend_kernel(scale, query_ref, key_ref, value_ref, limit_ref, out_ref):
    heads, rows, head_dim = query_ref.shape
    span = key_ref.shape[0]
    value_heads = key_ref.shape[1] // head_dim
    group = heads // value_heads
    devices = out_ref.shape[0]
    pairs = heads * rows // devices
    place = lax.broadcasted_iota(jnp.int32, (rows, span), 1)
    visible = (place < limit_ref[:, :1])[None]
    for g in range(value_heads):
        lanes = pl.ds(g * head_dim, head_dim)
        queries = query_ref[g * group : (g + 1) * group].reshape(group * rows, head_dim)
        logits = lax.dot_general(
            queries, key_ref[:, lanes], (((1,), (1,)), ((), ())),
            preferred_element_type=jnp.float32,
        ) * scale
        masked = jnp.where(visible, logits.reshape(group, rows, span), MASKED)
        top = jnp.max(masked, axis=2, keepdims=True)
        weights = jnp.where(visible, jnp.exp(masked - top), 0.0)
        total = jnp.sum(weights, axis=2, keepdims=True).reshape(group * rows, 1)
        top = top.reshape(group * rows, 1)
        summed = jnp.dot(
            weights.astype(jnp.bfloat16).reshape(group * rows, span), value_ref[:, lanes],
            preferred_element_type=jnp.float32,
        )
        seen = total > 0.0
        safe = jnp.where(seen, total, 1.0)
        means = (summed / safe).astype(jnp.bfloat16)
        level = jnp.where(seen, top + jnp.log(safe), MASKED)
        across = jnp.transpose(jnp.broadcast_to(level, (group * rows, LANES)))[:8]
        for first in range(0, group * rows, LANES):
            line = across[:, first : first + LANES]
            high = line.astype(jnp.bfloat16)
            rest = line - high.astype(jnp.float32)
            middle = rest.astype(jnp.bfloat16)
            low = (rest - middle.astype(jnp.float32)).astype(jnp.bfloat16)
            row = lax.broadcasted_iota(jnp.int32, line.shape, 0)
            terms = jnp.where(
                row == 0,
                high.astype(jnp.float32),
                jnp.where(row == 1, middle.astype(jnp.float32), low.astype(jnp.float32)),
            ).astype(jnp.bfloat16)
            for begin in range(0, LANES, pairs):
                index = (g * group * rows + first + begin) // pairs
                out_ref[index, :pairs] = means[first + begin : first + begin + pairs]
                out_ref[index, pairs:] = terms


def terms_of(level):
    line = jnp.transpose(level)[:8]
    high = line.astype(jnp.bfloat16).astype(jnp.float32)
    rest = line - high
    middle = rest.astype(jnp.bfloat16).astype(jnp.float32)
    row = lax.broadcasted_iota(jnp.int32, line.shape, 0)
    return jnp.where(row == 0, high, jnp.where(row == 1, middle, rest - middle)).astype(jnp.bfloat16)


def read_message(message):
    pairs = message.shape[0] - 8
    terms = message[pairs:].astype(jnp.float32)
    line = terms[0:1] + terms[1:2] + terms[2:3]
    return message[:pairs].astype(jnp.float32), jnp.transpose(jnp.broadcast_to(line, (LANES, LANES)))


def merge(parts):
    peak = parts[0][1]
    for _, level in parts[1:]:
        peak = jnp.maximum(peak, level)
    shares = [jnp.exp(level - peak) for _, level in parts]
    denominator = sum(shares[1:], shares[0])
    numerator = shares[0] * parts[0][0]
    for share, (mean, _) in zip(shares[1:], parts[1:]):
        numerator = numerator + share * mean
    return numerator / denominator, peak + jnp.log(denominator)


def put_message(message_ref, mean, level):
    pairs = mean.shape[0]
    message_ref[:pairs] = mean.astype(jnp.bfloat16)
    message_ref[pairs:] = terms_of(level)


def attend_unit_kernel(scale, head_dim, sends, device_ref, blocks_ref, key_ref, value_ref, limit_ref, *out_refs):
    value_heads, rows, _ = blocks_ref.shape
    span = value_ref.shape[0]
    local = LANES // (value_heads * rows)
    count = local * rows
    heads = value_heads * local
    group_index = lax.div(device_ref[0], lax.axis_size("ctx") // value_heads)
    limit = limit_ref[:, :1]
    visible = (lax.broadcasted_iota(jnp.int32, (rows, span), 1) < limit)[None]
    seen = jnp.broadcast_to((limit > 0)[None], (heads, rows, 1)).reshape(heads * rows, 1)
    logits = []
    for g in range(value_heads):
        block = blocks_ref[lax.bitwise_xor(group_index, g)]
        queries = jnp.concatenate(
            [block[:, h * head_dim : (h + 1) * head_dim] for h in range(local)], axis=0
        )
        logits.append(
            jnp.dot(
                queries, key_ref[g * head_dim : (g + 1) * head_dim, :],
                preferred_element_type=jnp.float32,
            )
        )
    logits = jnp.concatenate(logits, axis=0).reshape(heads, rows, span)
    masked = jnp.where(visible, logits, MASKED)
    top = jnp.max(masked, axis=2, keepdims=True)
    weights = jnp.exp2((masked - top) * (scale * math.log2(math.e)))
    total = jnp.sum(weights, axis=2, keepdims=True).reshape(heads * rows, 1)
    rounded = weights.astype(jnp.bfloat16).reshape(heads * rows, span)
    summed = jnp.concatenate(
        [
            jnp.dot(
                rounded[g * count : (g + 1) * count],
                value_ref[:, g * head_dim : (g + 1) * head_dim],
                preferred_element_type=jnp.float32,
            )
            for g in range(value_heads)
        ],
        axis=0,
    )
    mean = summed / total
    level = jnp.where(seen, top.reshape(heads * rows, 1) * scale + jnp.log(total), MASKED)
    level = jnp.broadcast_to(level, (heads * rows, LANES))
    if sends:
        put_message(out_refs[0], mean, level)
    else:
        out_refs[0][...] = mean
        out_refs[1][...] = level


def merge_last_kernel(mean_ref, level_ref, message_ref, sent_ref):
    mean, level = merge([(mean_ref[...], level_ref[...]), read_message(message_ref[...])])
    put_message(sent_ref, mean, level)


def merge_next_kernel(mean_ref, level_ref, core_ref, message_ref, sent_ref, mean_out_ref, level_out_ref):
    mean, level = merge(
        [(mean_ref[...], level_ref[...]), read_message(core_ref[...]), read_message(message_ref[...])]
    )
    put_message(sent_ref, mean, level)
    mean_out_ref[...] = mean
    level_out_ref[...] = level


def fresh_kernel(
    scale, head_dim, value_heads, key_width, device_ref, held_ref, brought_ref, far_ref, far_brought_ref,
    score_ref, value_ref,
):
    _, rows, used = far_ref.shape
    query_width = used - 2 * key_width
    run = head_dim // key_width
    group_index = lax.div(device_ref[0], run)
    core = lax.rem(device_ref[0], 2)
    step = lax.rem(lax.div(device_ref[0], 2), 2)
    for g in range(value_heads):
        turned = lax.bitwise_xor(group_index, g)
        news = []
        for index in range(run):
            same = core == index % 2
            block = jnp.where(
                step == index // 2,
                jnp.where(same, held_ref[turned], far_ref[turned]),
                jnp.where(same, brought_ref[turned], far_brought_ref[turned]),
            )
            news.append(block[:, query_width:])
        key = jnp.concatenate([new[:, :key_width] for new in news], axis=1).astype(jnp.float32)
        value = jnp.concatenate([new[:, key_width:] for new in news], axis=1).astype(jnp.float32)
        queries = far_ref[turned]
        for h in range(query_width // head_dim):
            query = queries[:, h * head_dim : (h + 1) * head_dim].astype(jnp.float32)
            score = jnp.sum(query * key, axis=1, keepdims=True) * scale
            span = pl.ds((g * (query_width // head_dim) + h) * rows, rows)
            score_ref[span, :] = jnp.broadcast_to(score, (rows, LANES))
            value_ref[span, :] = value


def settle_kernel(
    rows, mean_ref, level_ref, *refs
):
    *message_refs, score_ref, value_ref, out_ref = refs
    parts = [(mean_ref[...], level_ref[...])]
    parts += [read_message(message_ref[...]) for message_ref in message_refs]
    parts.append((value_ref[...], score_ref[...]))
    mean, _ = merge(parts)
    done = mean.astype(jnp.bfloat16)
    owners, _, width = out_ref.shape
    local = width // LANES
    for g in range(owners):
        first = g * local * rows
        out_ref[g] = jnp.concatenate(
            [done[first + h * rows : first + (h + 1) * rows] for h in range(local)], axis=1
        )


def residual_finish(factor, totals, extra_refs, out_ref):
    out_ref[...] = (extra_refs[0][...].astype(jnp.float32) + totals[0]).astype(jnp.bfloat16)


def by_group(device, place_index, devices):
    (stride, groups, _), (step, _, _), _ = digits(devices)
    place_in_group = lax.bitwise_xor(lax.rem(device, stride), 1)
    far = lax.div(place_index, devices // 2) if not isinstance(place_index, int) else place_index // (devices // 2)
    near_place = lax.rem(place_index, devices // 2)
    turned = lax.bitwise_xor(place_in_group, lax.div(near_place, groups) * step)
    return lax.rem(near_place, groups) * stride + lax.bitwise_xor(turned, far)


def order_kernel(device_ref, held_ref, out_ref):
    devices = held_ref.shape[0]

    def move(owner, carry):
        place = place_of(lax.bitwise_xor(device_ref[0], owner), devices)
        out_ref[owner] = held_ref[place]
        return carry

    lax.fori_loop(0, devices, move, 0, unroll=4)


def table_kernel(cos_ref, sin_ref, cos_out_ref, sin_out_ref):
    lane = lax.broadcasted_iota(jnp.int32, sin_ref.shape, 1)
    cos_out_ref[...] = cos_ref[...]
    sin_out_ref[...] = jnp.where(lane % 2 == 1, sin_ref[...], -sin_ref[...])


def finish_kernel(numerator_ref, denominator_ref, out_ref):
    out_ref[...] = (numerator_ref[...] / denominator_ref[...]).astype(jnp.bfloat16)


def output_kernel(blocks_ref, weight_ref, residual_ref, mid_ref, total):
    heads, _, head_dim = blocks_ref.shape
    total[...] = jnp.zeros_like(total)

    def step(index, carry):
        block = jnp.concatenate([blocks_ref[2 * index], blocks_ref[2 * index + 1]], axis=1)
        span = pl.ds(pl.multiple_of(index * 2 * head_dim, head_dim), 2 * head_dim)
        total[...] += jnp.dot(block, weight_ref[span, :], preferred_element_type=jnp.float32)
        return carry

    lax.fori_loop(0, heads // 2, step, 0, unroll=4)
    mid_ref[...] = (residual_ref[...].astype(jnp.float32) + total[...]).astype(jnp.bfloat16)


def rotation(first_col, width, positions, head_dim):
    col = jnp.arange(width, dtype=jnp.int32)
    in_head = ((first_col + col - col % 2) % head_dim).astype(jnp.float32)
    frequency = jnp.exp(-(in_head / head_dim) * jnp.log(jnp.float32(ROPE_BASE)))
    angles = positions.astype(jnp.float32)[:, None] * frequency[None, :]
    return jnp.cos(angles), jnp.sin(angles)


def shards(
    hidden_in,
    attn_gain,
    w_query,
    w_key,
    w_value,
    rotated_prefix_keys,
    cache_values,
    w_out,
    ffn_gain,
    w_gate,
    w_up,
    w_down,
    doc_offsets,
    slot_request,
):
    devices = lax.axis_size("ctx")
    device = lax.axis_index("ctx")
    own = lax.optimization_barrier(device.astype(jnp.int32)[None])
    rows, width = hidden_in.shape
    span, value_heads, head_dim = rotated_prefix_keys.shape
    query_width = w_query.shape[1]
    key_width = w_key.shape[1]
    heads = query_width * devices // head_dim
    group = heads // value_heads
    scale = 1.0 / math.sqrt(head_dim)
    slot_index = jnp.arange(rows, dtype=jnp.int32)
    positions = jnp.sum(
        jnp.where(slot_request[:, None] == slot_index[None, :], doc_offsets[None, :], 0), axis=1
    )

    def buffer(*shape, dtype=jnp.bfloat16):
        return jax.ShapeDtypeStruct(shape, dtype)

    def totals(*widths):
        return [pltpu.VMEM((rows, w), jnp.float32) for w in widths]

    used = query_width + 2 * key_width
    padded = -(-used // LANES) * LANES
    query_cos, query_sin = rotation(own * query_width, query_width, positions, head_dim)
    key_cos, key_sin = rotation(own * key_width, key_width, positions, head_dim)
    still = jnp.ones((rows, padded - query_width - key_width), jnp.float32)
    cosine = jnp.concatenate([query_cos, key_cos, still], axis=1)
    sine = jnp.concatenate([query_sin, key_sin, still * 0.0], axis=1)
    table = buffer(rows, padded, dtype=jnp.float32)
    cosine, sine = call(table_kernel, "table", (table, table), (cosine, sine), (), FLOPS["table"])
    begun = call(begin_kernel, "begin", buffer(rows, width), (own, hidden_in))
    sides = (w_key, w_value)
    if width % LANES == 0:
        sides = (w_key.T, w_value.T)
    projected = contract(
        "project", gathered(begun, hidden_in), own, (w_query, *sides), (query_width, key_width, key_width),
        attn_gain, project_finish, (cosine, sine), buffer(rows, used),
    )
    limit = jnp.broadcast_to((positions - own * span)[:, None], (rows, LANES))
    keys = rotated_prefix_keys.reshape(span, value_heads * head_dim)
    values = cache_values.reshape(span, value_heads * head_dim)
    rounds = digits(devices)
    if (
        len(rounds) == 3
        and rounds[0][1] == value_heads
        and rounds[1][1] == 2
        and head_dim == LANES
        and value_heads * (query_width // head_dim) * rows == LANES
    ):
        held, far, brought, far_brought = gathered(projected)
        unit = (LANES, LANES)
        message = buffer(LANES + 8, LANES)
        wide = buffer(*unit, dtype=jnp.float32)
        work = heads * rows * span * head_dim
        keys_across = rotated_prefix_keys.transpose(1, 2, 0).reshape(value_heads * head_dim, span)

        def attended(label, blocks, sends):
            return call(
                lambda *refs: attend_unit_kernel(scale, head_dim, sends, *refs), "attend_" + label,
                message if sends else (wide, wide), (own, blocks, keys_across, values, limit), (), work,
            )

        given = attended("a", held, True)
        taken_held = shifted(given, 1)
        mean, level = attended("b", far, False)
        given = attended("c", brought, True)
        taken = shifted(given, 1)
        given = call(
            merge_last_kernel, "merge_last", message, (*attended("d", far_brought, False), taken)
        )
        taken = shifted(given, rounds[1][0])
        given, mean, level = call(
            merge_next_kernel, "merge_next", (message, wide, wide), (mean, level, taken_held, taken)
        )
        taken = [shifted(given, rounds[0][0] * digit) for digit in range(1, rounds[0][1])]
        score, value = call(
            lambda *refs: fresh_kernel(scale, head_dim, value_heads, key_width, *refs), "fresh",
            (wide, wide), (own, held, brought, far, far_brought),
        )
        done = call(
            lambda *refs: settle_kernel(rows, *refs), "settle",
            buffer(value_heads, rows, query_width), (mean, level, *taken, score, value),
        )
        mid_part = contract(
            "output", pieces_of(done, *rounds[1][:2]), own, (w_out,), (width,),
            None, residual_finish, (hidden_in,), buffer(rows, width), by_group,
        )
    else:
        packed = exchange(jnp.broadcast_to(projected[None], (devices, rows, used)))

        def unpacked(first, part_width):
            part = packed[:, :, first : first + part_width]
            if part_width >= head_dim:
                split = part.reshape(devices, rows, part_width // head_dim, head_dim)
                return split.transpose(0, 2, 1, 3).reshape(-1, rows, head_dim)
            run = head_dim // part_width
            return part.reshape(-1, run, rows, part_width).transpose(0, 2, 1, 3).reshape(
                -1, rows, head_dim
            )

        queries = unpacked(0, query_width)
        key_new = unpacked(query_width, key_width)
        value_new = unpacked(query_width + key_width, key_width)
        pairs = heads * rows // devices
        sent = call(
            lambda *refs: attend_kernel(scale, *refs), "attend", buffer(devices, pairs + 8, LANES),
            (
                queries,
                keys,
                values,
                limit,
            ),
            (),
            4 * heads * rows * span * head_dim,
        )
        got = exchange(sent)
        first_pair = device * pairs
        means = got[:, :pairs].astype(jnp.float32)
        terms = lax.dynamic_slice_in_dim(
            got[:, pairs : pairs + 3].astype(jnp.float32), first_pair % LANES, pairs, 2
        )
        levels = terms[:, 0] + terms[:, 1] + terms[:, 2]

        def mine(every):
            return lax.dynamic_slice_in_dim(
                every.reshape(heads * rows, head_dim), first_pair, pairs, 0
            ).astype(jnp.float32)

        def spread(new):
            return jnp.broadcast_to(new[:, None], (value_heads, group, rows, head_dim))

        own_score = jnp.sum(mine(queries) * mine(spread(key_new)), axis=1) * scale
        own_value = mine(spread(value_new))
        peak = jnp.maximum(jnp.max(levels, axis=0), own_score)
        shares = jnp.exp(levels - peak[None, :])
        own_share = jnp.exp(own_score - peak)
        numerator = jnp.sum(shares[..., None] * means, axis=0) + own_share[:, None] * own_value
        denominator = jnp.sum(shares, axis=0) + own_share
        attn_part = call(
            finish_kernel, "finish", buffer(pairs, head_dim), (numerator, denominator[:, None]), (),
            FLOPS["finish"],
        )
        held = together(gathered(attn_part))
        attn_all = call(
            order_kernel, "order", buffer(devices, pairs, head_dim), (own, held)
        )
        mid_part = call(
            output_kernel, "output", buffer(rows, width),
            (attn_all.reshape(heads, rows, head_dim), w_out, hidden_in),
            totals(width),
            2 * rows * heads * head_dim * width,
        )
    hidden_width = w_gate.shape[1]
    hidden = contract(
        "gated", gathered(mid_part), own, (w_gate, w_up), (hidden_width, hidden_width),
        ffn_gain, gated_finish, (), buffer(rows, hidden_width),
    )
    hidden = call(begin_kernel, "relay", buffer(rows, hidden_width), (own, hidden))
    return contract(
        "down", gathered(hidden), own, (w_down,), (width,),
        None, down_finish, (mid_part,), buffer(rows, width),
    )


def solution(mesh):
    return jax.shard_map(
        shards,
        mesh=mesh,
        in_specs=(
            P("groups", "ctx"),
            P(),
            P(None, "ctx"),
            P(None, "ctx"),
            P(None, "ctx"),
            P(("groups", "ctx"), None, None),
            P(("groups", "ctx"), None, None),
            P(None, "ctx"),
            P(),
            P(None, "ctx"),
            P(None, "ctx"),
            P(None, "ctx"),
            P("groups"),
            P("groups"),
        ),
        out_specs=P("groups", "ctx"),
        check_vma=False,
    )
```

```python
import math

import jax
import jax.numpy as jnp
from jax import lax
from jax.experimental import pallas as pl
from jax.experimental.pallas import tpu as pltpu
from jax.sharding import PartitionSpec as P


NORM_EPSILON = 1e-05
ROPE_BASE = 500000.0
MASKED = -1e30


LANES = 128
FLOPS = {"begin": 10**11, "table": 10**11, "finish": 10**11, "output": 10**11, "relay": 10**11, "merge_next": 10**11, "output_a": 10**11}
VMEM = pl.BlockSpec(memory_space=pltpu.VMEM)
SMEM = pl.BlockSpec(memory_space=pltpu.SMEM)


def exchange(blocks):
    return lax.all_to_all(blocks, "ctx", 0, 0)


def digits(devices):
    rest, stride, place, out = devices // 2, devices, 1, []
    while rest > 1:
        radix = 4 if rest % 4 == 0 else 2
        stride //= radix
        out.append((stride, radix, place))
        place *= radix
        rest //= radix
    return out + [(1, 2, place)]


def mask_at(place_index, devices):
    return sum(((place_index // place) % radix) * stride for stride, radix, place in digits(devices))


def place_of(mask, devices):
    return sum(((mask // stride) % radix) * place for stride, radix, place in digits(devices))


def shifted(part, mask):
    devices = lax.axis_size("ctx")
    return lax.ppermute(part, "ctx", [(index, index ^ mask) for index in range(devices)])


def gathered(part, given=None):
    devices = lax.axis_size("ctx")
    held = part[None]
    *rounds, last, _ = digits(devices)

    def arrive(stride, radix, held):
        out = {}
        for digit in sorted(range(1, radix), key=lambda d: ((3,2,1))[d - 1]):
            out[digit] = shifted(held, stride * digit)
        return [out[digit] for digit in range(1, radix)]

    for stride, radix, _ in rounds:
        arrived = arrive(stride, radix, held if given is None else given[None])
        given = None
        held = jnp.concatenate([held] + arrived, axis=0)
    return pieces_of(held, *last[:2])


def pieces_of(held, stride, radix):
    brought = [shifted(held, stride * digit) for digit in range(1, radix)]
    brought = brought[0] if radix == 2 else jnp.concatenate(brought, axis=0)
    far = shifted(held, 1)
    return held, far, brought, shifted(brought, 1)


def together(pieces):
    held, far, brought, far_brought = pieces
    return jnp.concatenate([held, brought, far, far_brought], axis=0)


def call(body, name, out_shape, args, scratch=(), flops=0):
    moved = sum(a.size * a.dtype.itemsize for a in args)
    return pl.pallas_call(
        body,
        out_shape=out_shape,
        in_specs=[SMEM if a.dtype == jnp.int32 and a.ndim == 1 else VMEM for a in args],
        out_specs=jax.tree.map(lambda _: VMEM, out_shape),
        scratch_shapes=list(scratch),
        compiler_params=pltpu.CompilerParams(vmem_limit_bytes=6 << 20),
        cost_estimate=pl.CostEstimate(flops=FLOPS.get(name, flops), bytes_accessed=moved, transcendentals=0),
    )(*args)


def accumulate(device_ref, devices, pieces, owner_of, gain_ref, weight_refs, total_refs, square_ref):
    for first, piece_ref in pieces:
        places, _, depth = piece_ref.shape

        def step(index, carry):
            owner = owner_of(device_ref[0], first + index, devices)
            block = piece_ref[index]
            if gain_ref is not None:
                wide = block.astype(jnp.float32)
                block = (wide * gain_ref[owner]).astype(jnp.bfloat16)
                square_ref[...] += sum(
                    wide[:, lane : lane + LANES] * wide[:, lane : lane + LANES]
                    for lane in range(0, depth, LANES)
                ) if depth % LANES == 0 else jnp.broadcast_to(
                    jnp.sum(wide * wide, axis=1, keepdims=True) / LANES, square_ref.shape
                )
            span = pl.ds(pl.multiple_of(owner * depth, depth), depth)
            for weight_ref, total_ref in zip(weight_refs, total_refs):
                if weight_ref.shape[1] == devices * depth:
                    total_ref[...] += lax.dot_general(
                        block, weight_ref[:, span], (((1,), (1,)), ((), ())),
                        preferred_element_type=jnp.float32,
                    )
                else:
                    total_ref[...] += jnp.dot(
                        block, weight_ref[span, :], preferred_element_type=jnp.float32
                    )
            return carry

        lax.fori_loop(0, places, step, 0, unroll=4)


def by_place(device, place_index, devices):
    return lax.bitwise_xor(device, mask_at(place_index, devices))


def contract(name, pieces, own, weights, widths, gain, finish, extras, out_shape, owner_of=by_place):
    devices = lax.axis_size("ctx")
    near, rows, depth = pieces[0].shape
    normed = gain is not None
    gains = [gain.reshape(devices, 1, depth)] if normed else []
    totals_of = [jax.ShapeDtypeStruct((rows, w), jnp.float32) for w in widths]
    if normed:
        totals_of.append(jax.ShapeDtypeStruct((rows, LANES), jnp.float32))
    scratch = [pltpu.VMEM(t.shape, t.dtype) for t in totals_of]

    def stage(label, first, parts, before, last):
        def kernel(device_ref, *refs):
            refs = list(refs)
            take = lambda count: [refs.pop(0) for _ in range(count)]
            part_refs, gain_refs, weight_refs = take(len(parts)), take(len(gains)), take(len(weights))
            before_refs = take(len(before))
            extra_refs = take(len(extras)) if last else []
            out_refs = take(1 if last else 0)
            total_refs = refs
            for index, total_ref in enumerate(total_refs):
                if before:
                    total_ref[...] = before_refs[index][...]
                else:
                    total_ref[...] = jnp.zeros_like(total_ref)
            place, placed = first, []
            for part_ref in part_refs:
                placed.append((place, part_ref))
                place += part_ref.shape[0]
            accumulate(
                device_ref, devices, placed, owner_of, gain_refs[0] if normed else None,
                weight_refs, total_refs[: len(weights)], total_refs[-1],
            )
            if last:
                factor = None
                if normed:
                    mean = jnp.sum(total_refs[-1][...], axis=1, keepdims=True) / (devices * depth)
                    factor = lax.rsqrt(mean + NORM_EPSILON)
                finish(factor, [t[...] for t in total_refs[: len(weights)]], extra_refs, out_refs[0])

        return call(
            kernel, name + label, out_shape if last else tuple(totals_of),
            (own, *parts, *gains, *weights, *before, *(extras if last else ())),
            scratch if last else (),
            2 * rows * sum(p.shape[0] for p in parts) * depth * sum(widths),
        )

    sums = ()
    firsts = (0, devices // 2, near, devices // 2 + near)
    for label, first, piece in zip(("_a", "_b", "_c", "_d"), firsts, pieces):
        sums = stage(label, first, [piece], sums, label == "_d")
    return sums


def project_finish(factor, totals, extra_refs, out_ref):
    cos_ref, sin_ref = extra_refs
    query, key, value = (factor * total for total in totals)
    query_width = query.shape[1]
    key_width = key.shape[1]
    used = query_width + 2 * key_width
    columns = jnp.concatenate(
        [query, key, value, jnp.zeros((query.shape[0], cos_ref.shape[1] - used), jnp.float32)], axis=1
    )
    width = columns.shape[1]
    lane = lax.broadcasted_iota(jnp.int32, columns.shape, 1)
    partner = jnp.where(
        lane % 2 == 1, pltpu.roll(columns, 1, 1), pltpu.roll(columns, width - 1, 1)
    )
    turned = columns * cos_ref[...] + partner * sin_ref[...]
    out_ref[...] = turned.astype(jnp.bfloat16)[:, :used]


def gated_finish(factor, totals, extra_refs, out_ref):
    gate, up = (factor * total for total in totals)
    out_ref[...] = (gate / (1.0 + jnp.exp(-gate)) * up).astype(jnp.bfloat16)


def down_finish(factor, totals, extra_refs, out_ref):
    out_ref[...] = (extra_refs[0][...].astype(jnp.float32) + totals[0]).astype(jnp.bfloat16)


def begin_kernel(device_ref, in_ref, out_ref):
    out_ref[...] = in_ref[...]


def attend_kernel(scale, query_ref, key_ref, value_ref, limit_ref, out_ref):
    heads, rows, head_dim = query_ref.shape
    span = key_ref.shape[0]
    value_heads = key_ref.shape[1] // head_dim
    group = heads // value_heads
    devices = out_ref.shape[0]
    pairs = heads * rows // devices
    place = lax.broadcasted_iota(jnp.int32, (rows, span), 1)
    visible = (place < limit_ref[:, :1])[None]
    for g in range(value_heads):
        lanes = pl.ds(g * head_dim, head_dim)
        queries = query_ref[g * group : (g + 1) * group].reshape(group * rows, head_dim)
        logits = lax.dot_general(
            queries, key_ref[:, lanes], (((1,), (1,)), ((), ())),
            preferred_element_type=jnp.float32,
        ) * scale
        masked = jnp.where(visible, logits.reshape(group, rows, span), MASKED)
        top = jnp.max(masked, axis=2, keepdims=True)
        weights = jnp.where(visible, jnp.exp(masked - top), 0.0)
        total = jnp.sum(weights, axis=2, keepdims=True).reshape(group * rows, 1)
        top = top.reshape(group * rows, 1)
        summed = jnp.dot(
            weights.astype(jnp.bfloat16).reshape(group * rows, span), value_ref[:, lanes],
            preferred_element_type=jnp.float32,
        )
        seen = total > 0.0
        safe = jnp.where(seen, total, 1.0)
        means = (summed / safe).astype(jnp.bfloat16)
        level = jnp.where(seen, top + jnp.log(safe), MASKED)
        across = jnp.transpose(jnp.broadcast_to(level, (group * rows, LANES)))[:8]
        for first in range(0, group * rows, LANES):
            line = across[:, first : first + LANES]
            high = line.astype(jnp.bfloat16)
            rest = line - high.astype(jnp.float32)
            middle = rest.astype(jnp.bfloat16)
            low = (rest - middle.astype(jnp.float32)).astype(jnp.bfloat16)
            row = lax.broadcasted_iota(jnp.int32, line.shape, 0)
            terms = jnp.where(
                row == 0,
                high.astype(jnp.float32),
                jnp.where(row == 1, middle.astype(jnp.float32), low.astype(jnp.float32)),
            ).astype(jnp.bfloat16)
            for begin in range(0, LANES, pairs):
                index = (g * group * rows + first + begin) // pairs
                out_ref[index, :pairs] = means[first + begin : first + begin + pairs]
                out_ref[index, pairs:] = terms


def terms_of(level):
    line = jnp.transpose(level)[:8]
    high = line.astype(jnp.bfloat16).astype(jnp.float32)
    rest = line - high
    middle = rest.astype(jnp.bfloat16).astype(jnp.float32)
    row = lax.broadcasted_iota(jnp.int32, line.shape, 0)
    return jnp.where(row == 0, high, jnp.where(row == 1, middle, rest - middle)).astype(jnp.bfloat16)


def read_message(message):
    pairs = message.shape[0] - 8
    terms = message[pairs:].astype(jnp.float32)
    line = terms[0:1] + terms[1:2] + terms[2:3]
    return message[:pairs].astype(jnp.float32), jnp.transpose(jnp.broadcast_to(line, (LANES, LANES)))


def merge(parts):
    peak = parts[0][1]
    for _, level in parts[1:]:
        peak = jnp.maximum(peak, level)
    shares = [jnp.exp(level - peak) for _, level in parts]
    denominator = sum(shares[1:], shares[0])
    numerator = shares[0] * parts[0][0]
    for share, (mean, _) in zip(shares[1:], parts[1:]):
        numerator = numerator + share * mean
    return numerator / denominator, peak + jnp.log(denominator)


def put_message(message_ref, mean, level):
    pairs = mean.shape[0]
    message_ref[:pairs] = mean.astype(jnp.bfloat16)
    message_ref[pairs:] = terms_of(level)


def attend_unit_kernel(scale, head_dim, sends, device_ref, blocks_ref, key_ref, value_ref, limit_ref, *out_refs):
    value_heads, rows, _ = blocks_ref.shape
    span = value_ref.shape[0]
    local = LANES // (value_heads * rows)
    count = local * rows
    heads = value_heads * local
    group_index = lax.div(device_ref[0], lax.axis_size("ctx") // value_heads)
    limit = limit_ref[:, :1]
    visible = (lax.broadcasted_iota(jnp.int32, (rows, span), 1) < limit)[None]
    seen = jnp.broadcast_to((limit > 0)[None], (heads, rows, 1)).reshape(heads * rows, 1)
    logits = []
    for g in range(value_heads):
        block = blocks_ref[lax.bitwise_xor(group_index, g)]
        queries = jnp.concatenate(
            [block[:, h * head_dim : (h + 1) * head_dim] for h in range(local)], axis=0
        )
        logits.append(
            jnp.dot(
                queries, key_ref[g * head_dim : (g + 1) * head_dim, :],
                preferred_element_type=jnp.float32,
            )
        )
    logits = jnp.concatenate(logits, axis=0).reshape(heads, rows, span)
    masked = jnp.where(visible, logits, MASKED)
    top = jnp.max(masked, axis=2, keepdims=True)
    weights = jnp.exp2((masked - top) * (scale * math.log2(math.e)))
    total = jnp.sum(weights, axis=2, keepdims=True).reshape(heads * rows, 1)
    rounded = weights.astype(jnp.bfloat16).reshape(heads * rows, span)
    summed = jnp.concatenate(
        [
            jnp.dot(
                rounded[g * count : (g + 1) * count],
                value_ref[:, g * head_dim : (g + 1) * head_dim],
                preferred_element_type=jnp.float32,
            )
            for g in range(value_heads)
        ],
        axis=0,
    )
    mean = summed / total
    level = jnp.where(seen, top.reshape(heads * rows, 1) * scale + jnp.log(total), MASKED)
    level = jnp.broadcast_to(level, (heads * rows, LANES))
    if sends:
        put_message(out_refs[0], mean, level)
    else:
        out_refs[0][...] = mean
        out_refs[1][...] = level


def merge_last_kernel(mean_ref, level_ref, message_ref, sent_ref):
    mean, level = merge([(mean_ref[...], level_ref[...]), read_message(message_ref[...])])
    put_message(sent_ref, mean, level)


def merge_next_kernel(mean_ref, level_ref, core_ref, message_ref, sent_ref, mean_out_ref, level_out_ref):
    mean, level = merge(
        [(mean_ref[...], level_ref[...]), read_message(core_ref[...]), read_message(message_ref[...])]
    )
    put_message(sent_ref, mean, level)
    mean_out_ref[...] = mean
    level_out_ref[...] = level


def fresh_kernel(
    scale, head_dim, value_heads, key_width, device_ref, held_ref, brought_ref, far_ref, far_brought_ref,
    score_ref, value_ref,
):
    _, rows, used = far_ref.shape
    query_width = used - 2 * key_width
    run = head_dim // key_width
    group_index = lax.div(device_ref[0], run)
    core = lax.rem(device_ref[0], 2)
    step = lax.rem(lax.div(device_ref[0], 2), 2)
    for g in range(value_heads):
        turned = lax.bitwise_xor(group_index, g)
        news = []
        for index in range(run):
            same = core == index % 2
            block = jnp.where(
                step == index // 2,
                jnp.where(same, held_ref[turned], far_ref[turned]),
                jnp.where(same, brought_ref[turned], far_brought_ref[turned]),
            )
            news.append(block[:, query_width:])
        key = jnp.concatenate([new[:, :key_width] for new in news], axis=1).astype(jnp.float32)
        value = jnp.concatenate([new[:, key_width:] for new in news], axis=1).astype(jnp.float32)
        queries = far_ref[turned]
        for h in range(query_width // head_dim):
            query = queries[:, h * head_dim : (h + 1) * head_dim].astype(jnp.float32)
            score = jnp.sum(query * key, axis=1, keepdims=True) * scale
            span = pl.ds((g * (query_width // head_dim) + h) * rows, rows)
            score_ref[span, :] = jnp.broadcast_to(score, (rows, LANES))
            value_ref[span, :] = value


def settle_kernel(
    rows, mean_ref, level_ref, *refs
):
    *message_refs, score_ref, value_ref, out_ref = refs
    parts = [(mean_ref[...], level_ref[...])]
    parts += [read_message(message_ref[...]) for message_ref in message_refs]
    parts.append((value_ref[...], score_ref[...]))
    mean, _ = merge(parts)
    done = mean.astype(jnp.bfloat16)
    owners, _, width = out_ref.shape
    local = width // LANES
    for g in range(owners):
        first = g * local * rows
        out_ref[g] = jnp.concatenate(
            [done[first + h * rows : first + (h + 1) * rows] for h in range(local)], axis=1
        )


def residual_finish(factor, totals, extra_refs, out_ref):
    out_ref[...] = (extra_refs[0][...].astype(jnp.float32) + totals[0]).astype(jnp.bfloat16)


def by_group(device, place_index, devices):
    (stride, groups, _), (step, _, _), _ = digits(devices)
    place_in_group = lax.bitwise_xor(lax.rem(device, stride), 1)
    far = lax.div(place_index, devices // 2) if not isinstance(place_index, int) else place_index // (devices // 2)
    near_place = lax.rem(place_index, devices // 2)
    turned = lax.bitwise_xor(place_in_group, lax.div(near_place, groups) * step)
    return lax.rem(near_place, groups) * stride + lax.bitwise_xor(turned, far)


def order_kernel(device_ref, held_ref, out_ref):
    devices = held_ref.shape[0]

    def move(owner, carry):
        place = place_of(lax.bitwise_xor(device_ref[0], owner), devices)
        out_ref[owner] = held_ref[place]
        return carry

    lax.fori_loop(0, devices, move, 0, unroll=4)


def table_kernel(cos_ref, sin_ref, cos_out_ref, sin_out_ref):
    lane = lax.broadcasted_iota(jnp.int32, sin_ref.shape, 1)
    cos_out_ref[...] = cos_ref[...]
    sin_out_ref[...] = jnp.where(lane % 2 == 1, sin_ref[...], -sin_ref[...])


def finish_kernel(numerator_ref, denominator_ref, out_ref):
    out_ref[...] = (numerator_ref[...] / denominator_ref[...]).astype(jnp.bfloat16)


def output_kernel(blocks_ref, weight_ref, residual_ref, mid_ref, total):
    heads, _, head_dim = blocks_ref.shape
    total[...] = jnp.zeros_like(total)

    def step(index, carry):
        block = jnp.concatenate([blocks_ref[2 * index], blocks_ref[2 * index + 1]], axis=1)
        span = pl.ds(pl.multiple_of(index * 2 * head_dim, head_dim), 2 * head_dim)
        total[...] += jnp.dot(block, weight_ref[span, :], preferred_element_type=jnp.float32)
        return carry

    lax.fori_loop(0, heads // 2, step, 0, unroll=4)
    mid_ref[...] = (residual_ref[...].astype(jnp.float32) + total[...]).astype(jnp.bfloat16)


def rotation(first_col, width, positions, head_dim):
    col = jnp.arange(width, dtype=jnp.int32)
    in_head = ((first_col + col - col % 2) % head_dim).astype(jnp.float32)
    frequency = jnp.exp(-(in_head / head_dim) * jnp.log(jnp.float32(ROPE_BASE)))
    angles = positions.astype(jnp.float32)[:, None] * frequency[None, :]
    return jnp.cos(angles), jnp.sin(angles)


def shards(
    hidden_in,
    attn_gain,
    w_query,
    w_key,
    w_value,
    rotated_prefix_keys,
    cache_values,
    w_out,
    ffn_gain,
    w_gate,
    w_up,
    w_down,
    doc_offsets,
    slot_request,
):
    devices = lax.axis_size("ctx")
    device = lax.axis_index("ctx")
    own = lax.optimization_barrier(device.astype(jnp.int32)[None])
    rows, width = hidden_in.shape
    span, value_heads, head_dim = rotated_prefix_keys.shape
    query_width = w_query.shape[1]
    key_width = w_key.shape[1]
    heads = query_width * devices // head_dim
    group = heads // value_heads
    scale = 1.0 / math.sqrt(head_dim)
    slot_index = jnp.arange(rows, dtype=jnp.int32)
    positions = jnp.sum(
        jnp.where(slot_request[:, None] == slot_index[None, :], doc_offsets[None, :], 0), axis=1
    )

    def buffer(*shape, dtype=jnp.bfloat16):
        return jax.ShapeDtypeStruct(shape, dtype)

    def totals(*widths):
        return [pltpu.VMEM((rows, w), jnp.float32) for w in widths]

    used = query_width + 2 * key_width
    padded = -(-used // LANES) * LANES
    query_cos, query_sin = rotation(own * query_width, query_width, positions, head_dim)
    key_cos, key_sin = rotation(own * key_width, key_width, positions, head_dim)
    still = jnp.ones((rows, padded - query_width - key_width), jnp.float32)
    cosine = jnp.concatenate([query_cos, key_cos, still], axis=1)
    sine = jnp.concatenate([query_sin, key_sin, still * 0.0], axis=1)
    table = buffer(rows, padded, dtype=jnp.float32)
    cosine, sine = call(table_kernel, "table", (table, table), (cosine, sine), (), FLOPS["table"])
    begun = call(begin_kernel, "begin", buffer(rows, width), (own, hidden_in))
    sides = (w_key, w_value)
    if width % LANES == 0:
        sides = (w_key.T, w_value.T)
    projected = contract(
        "project", gathered(begun, hidden_in), own, (w_query, *sides), (query_width, key_width, key_width),
        attn_gain, project_finish, (cosine, sine), buffer(rows, used),
    )
    limit = jnp.broadcast_to((positions - own * span)[:, None], (rows, LANES))
    keys = rotated_prefix_keys.reshape(span, value_heads * head_dim)
    values = cache_values.reshape(span, value_heads * head_dim)
    rounds = digits(devices)
    if (
        len(rounds) == 3
        and rounds[0][1] == value_heads
        and rounds[1][1] == 2
        and head_dim == LANES
        and value_heads * (query_width // head_dim) * rows == LANES
    ):
        held, far, brought, far_brought = gathered(projected)
        unit = (LANES, LANES)
        message = buffer(LANES + 8, LANES)
        wide = buffer(*unit, dtype=jnp.float32)
        work = heads * rows * span * head_dim
        keys_across = rotated_prefix_keys.transpose(1, 2, 0).reshape(value_heads * head_dim, span)

        def attended(label, blocks, sends):
            return call(
                lambda *refs: attend_unit_kernel(scale, head_dim, sends, *refs), "attend_" + label,
                message if sends else (wide, wide), (own, blocks, keys_across, values, limit), (), work,
            )

        given = attended("a", held, True)
        taken_held = shifted(given, 1)
        mean, level = attended("b", far, False)
        given = attended("c", brought, True)
        taken = shifted(given, 1)
        given = call(
            merge_last_kernel, "merge_last", message, (*attended("d", far_brought, False), taken)
        )
        taken = shifted(given, rounds[1][0])
        given, mean, level = call(
            merge_next_kernel, "merge_next", (message, wide, wide), (mean, level, taken_held, taken)
        )
        taken = []
        for digit in range(1, rounds[0][1]):
            taken.append(shifted(given, rounds[0][0] * digit))
        score, value = call(
            lambda *refs: fresh_kernel(scale, head_dim, value_heads, key_width, *refs), "fresh",
            (wide, wide), (own, held, brought, far, far_brought),
        )
        done = call(
            lambda *refs: settle_kernel(rows, *refs), "settle",
            buffer(value_heads, rows, query_width), (mean, level, *taken, score, value),
        )
        mid_part = contract(
            "output", pieces_of(done, *rounds[1][:2]), own, (w_out,), (width,),
            None, residual_finish, (hidden_in,), buffer(rows, width), by_group,
        )
    else:
        packed = exchange(jnp.broadcast_to(projected[None], (devices, rows, used)))

        def unpacked(first, part_width):
            part = packed[:, :, first : first + part_width]
            if part_width >= head_dim:
                split = part.reshape(devices, rows, part_width // head_dim, head_dim)
                return split.transpose(0, 2, 1, 3).reshape(-1, rows, head_dim)
            run = head_dim // part_width
            return part.reshape(-1, run, rows, part_width).transpose(0, 2, 1, 3).reshape(
                -1, rows, head_dim
            )

        queries = unpacked(0, query_width)
        key_new = unpacked(query_width, key_width)
        value_new = unpacked(query_width + key_width, key_width)
        pairs = heads * rows // devices
        sent = call(
            lambda *refs: attend_kernel(scale, *refs), "attend", buffer(devices, pairs + 8, LANES),
            (
                queries,
                keys,
                values,
                limit,
            ),
            (),
            4 * heads * rows * span * head_dim,
        )
        got = exchange(sent)
        first_pair = device * pairs
        means = got[:, :pairs].astype(jnp.float32)
        terms = lax.dynamic_slice_in_dim(
            got[:, pairs : pairs + 3].astype(jnp.float32), first_pair % LANES, pairs, 2
        )
        levels = terms[:, 0] + terms[:, 1] + terms[:, 2]

        def mine(every):
            return lax.dynamic_slice_in_dim(
                every.reshape(heads * rows, head_dim), first_pair, pairs, 0
            ).astype(jnp.float32)

        def spread(new):
            return jnp.broadcast_to(new[:, None], (value_heads, group, rows, head_dim))

        own_score = jnp.sum(mine(queries) * mine(spread(key_new)), axis=1) * scale
        own_value = mine(spread(value_new))
        peak = jnp.maximum(jnp.max(levels, axis=0), own_score)
        shares = jnp.exp(levels - peak[None, :])
        own_share = jnp.exp(own_score - peak)
        numerator = jnp.sum(shares[..., None] * means, axis=0) + own_share[:, None] * own_value
        denominator = jnp.sum(shares, axis=0) + own_share
        attn_part = call(
            finish_kernel, "finish", buffer(pairs, head_dim), (numerator, denominator[:, None]), (),
            FLOPS["finish"],
        )
        held = together(gathered(attn_part))
        attn_all = call(
            order_kernel, "order", buffer(devices, pairs, head_dim), (own, held)
        )
        mid_part = call(
            output_kernel, "output", buffer(rows, width),
            (attn_all.reshape(heads, rows, head_dim), w_out, hidden_in),
            totals(width),
            2 * rows * heads * head_dim * width,
        )
    hidden_width = w_gate.shape[1]
    hidden = contract(
        "gated", gathered(mid_part), own, (w_gate, w_up), (hidden_width, hidden_width),
        ffn_gain, gated_finish, (), buffer(rows, hidden_width),
    )
    hidden = call(begin_kernel, "relay", buffer(rows, hidden_width), (own, hidden))
    return contract(
        "down", gathered(hidden), own, (w_down,), (width,),
        None, down_finish, (mid_part,), buffer(rows, width),
    )


def solution(mesh):
    return jax.shard_map(
        shards,
        mesh=mesh,
        in_specs=(
            P("groups", "ctx"),
            P(),
            P(None, "ctx"),
            P(None, "ctx"),
            P(None, "ctx"),
            P(("groups", "ctx"), None, None),
            P(("groups", "ctx"), None, None),
            P(None, "ctx"),
            P(),
            P(None, "ctx"),
            P(None, "ctx"),
            P(None, "ctx"),
            P("groups"),
            P("groups"),
        ),
        out_specs=P("groups", "ctx"),
        check_vma=False,
    )
```

```python
import math

import jax
import jax.numpy as jnp
from jax import lax
from jax.experimental import pallas as pl
from jax.experimental.pallas import tpu as pltpu
from jax.sharding import PartitionSpec as P


NORM_EPSILON = 1e-05
ROPE_BASE = 500000.0
MASKED = -1e30


LANES = 128
FLOPS = {"begin": 10**11, "table": 10**11, "finish": 10**11, "output": 10**11, "relay": 10**11, "merge_next": 10**11, "output_a": 10**11}
VMEM = pl.BlockSpec(memory_space=pltpu.VMEM)
SMEM = pl.BlockSpec(memory_space=pltpu.SMEM)


def exchange(blocks):
    return lax.all_to_all(blocks, "ctx", 0, 0)


def digits(devices):
    rest, stride, place, out = devices // 2, devices, 1, []
    while rest > 1:
        radix = 4 if rest % 4 == 0 else 2
        stride //= radix
        out.append((stride, radix, place))
        place *= radix
        rest //= radix
    return out + [(1, 2, place)]


def mask_at(place_index, devices):
    return sum(((place_index // place) % radix) * stride for stride, radix, place in digits(devices))


def place_of(mask, devices):
    return sum(((mask // stride) % radix) * place for stride, radix, place in digits(devices))


def shifted(part, mask):
    devices = lax.axis_size("ctx")
    return lax.ppermute(part, "ctx", [(index, index ^ mask) for index in range(devices)])


def gathered(part, given=None):
    devices = lax.axis_size("ctx")
    held = part[None]
    *rounds, last, _ = digits(devices)

    def arrive(stride, radix, held):
        out = {}
        for digit in sorted(range(1, radix), key=lambda d: ((3,2,1))[d - 1]):
            out[digit] = shifted(held, stride * digit)
        return [out[digit] for digit in range(1, radix)]

    for stride, radix, _ in rounds:
        arrived = arrive(stride, radix, held if given is None else given[None])
        given = None
        held = jnp.concatenate([held] + arrived, axis=0)
    return pieces_of(held, *last[:2])


def pieces_of(held, stride, radix):
    brought = [shifted(held, stride * digit) for digit in range(1, radix)]
    brought = brought[0] if radix == 2 else jnp.concatenate(brought, axis=0)
    far = shifted(held, 1)
    return held, far, brought, shifted(brought, 1)


def together(pieces):
    held, far, brought, far_brought = pieces
    return jnp.concatenate([held, brought, far, far_brought], axis=0)


def call(body, name, out_shape, args, scratch=(), flops=0):
    moved = sum(a.size * a.dtype.itemsize for a in args)
    return pl.pallas_call(
        body,
        out_shape=out_shape,
        in_specs=[SMEM if a.dtype == jnp.int32 and a.ndim == 1 else VMEM for a in args],
        out_specs=jax.tree.map(lambda _: VMEM, out_shape),
        scratch_shapes=list(scratch),
        compiler_params=pltpu.CompilerParams(vmem_limit_bytes=6 << 20),
        cost_estimate=pl.CostEstimate(flops=FLOPS.get(name, flops), bytes_accessed=moved, transcendentals=0),
    )(*args)


def accumulate(device_ref, devices, pieces, owner_of, gain_ref, weight_refs, total_refs, square_ref):
    for first, piece_ref in pieces:
        places, _, depth = piece_ref.shape

        def step(index, carry):
            owner = owner_of(device_ref[0], first + index, devices)
            block = piece_ref[index]
            if gain_ref is not None:
                wide = block.astype(jnp.float32)
                block = (wide * gain_ref[owner]).astype(jnp.bfloat16)
                square_ref[...] += sum(
                    wide[:, lane : lane + LANES] * wide[:, lane : lane + LANES]
                    for lane in range(0, depth, LANES)
                ) if depth % LANES == 0 else jnp.broadcast_to(
                    jnp.sum(wide * wide, axis=1, keepdims=True) / LANES, square_ref.shape
                )
            span = pl.ds(pl.multiple_of(owner * depth, depth), depth)
            for weight_ref, total_ref in zip(weight_refs, total_refs):
                if weight_ref.shape[1] == devices * depth:
                    total_ref[...] += lax.dot_general(
                        block, weight_ref[:, span], (((1,), (1,)), ((), ())),
                        preferred_element_type=jnp.float32,
                    )
                else:
                    total_ref[...] += jnp.dot(
                        block, weight_ref[span, :], preferred_element_type=jnp.float32
                    )
            return carry

        lax.fori_loop(0, places, step, 0, unroll=4)


def by_place(device, place_index, devices):
    return lax.bitwise_xor(device, mask_at(place_index, devices))


def contract(name, pieces, own, weights, widths, gain, finish, extras, out_shape, owner_of=by_place):
    devices = lax.axis_size("ctx")
    near, rows, depth = pieces[0].shape
    normed = gain is not None
    gains = [gain.reshape(devices, 1, depth)] if normed else []
    totals_of = [jax.ShapeDtypeStruct((rows, w), jnp.float32) for w in widths]
    if normed:
        totals_of.append(jax.ShapeDtypeStruct((rows, LANES), jnp.float32))
    scratch = [pltpu.VMEM(t.shape, t.dtype) for t in totals_of]

    def stage(label, first, parts, before, last):
        def kernel(device_ref, *refs):
            refs = list(refs)
            take = lambda count: [refs.pop(0) for _ in range(count)]
            part_refs, gain_refs, weight_refs = take(len(parts)), take(len(gains)), take(len(weights))
            before_refs = take(len(before))
            extra_refs = take(len(extras)) if last else []
            out_refs = take(1 if last else 0)
            total_refs = refs
            for index, total_ref in enumerate(total_refs):
                if before:
                    total_ref[...] = before_refs[index][...]
                else:
                    total_ref[...] = jnp.zeros_like(total_ref)
            place, placed = first, []
            for part_ref in part_refs:
                placed.append((place, part_ref))
                place += part_ref.shape[0]
            accumulate(
                device_ref, devices, placed, owner_of, gain_refs[0] if normed else None,
                weight_refs, total_refs[: len(weights)], total_refs[-1],
            )
            if last:
                factor = None
                if normed:
                    mean = jnp.sum(total_refs[-1][...], axis=1, keepdims=True) / (devices * depth)
                    factor = lax.rsqrt(mean + NORM_EPSILON)
                finish(factor, [t[...] for t in total_refs[: len(weights)]], extra_refs, out_refs[0])

        return call(
            kernel, name + label, out_shape if last else tuple(totals_of),
            (own, *parts, *gains, *weights, *before, *(extras if last else ())),
            scratch if last else (),
            2 * rows * sum(p.shape[0] for p in parts) * depth * sum(widths),
        )

    sums = ()
    firsts = (0, devices // 2, near, devices // 2 + near)
    for label, first, piece in zip(("_a", "_b", "_c", "_d"), firsts, pieces):
        sums = stage(label, first, [piece], sums, label == "_d")
    return sums


def project_finish(factor, totals, extra_refs, out_ref):
    cos_ref, sin_ref = extra_refs
    query, key, value = (factor * total for total in totals)
    query_width = query.shape[1]
    key_width = key.shape[1]
    used = query_width + 2 * key_width
    columns = jnp.concatenate(
        [query, key, value, jnp.zeros((query.shape[0], cos_ref.shape[1] - used), jnp.float32)], axis=1
    )
    width = columns.shape[1]
    lane = lax.broadcasted_iota(jnp.int32, columns.shape, 1)
    partner = jnp.where(
        lane % 2 == 1, pltpu.roll(columns, 1, 1), pltpu.roll(columns, width - 1, 1)
    )
    turned = columns * cos_ref[...] + partner * sin_ref[...]
    out_ref[...] = turned.astype(jnp.bfloat16)[:, :used]


def gated_finish(factor, totals, extra_refs, out_ref):
    gate, up = (factor * total for total in totals)
    out_ref[...] = (gate / (1.0 + jnp.exp(-gate)) * up).astype(jnp.bfloat16)


def down_finish(factor, totals, extra_refs, out_ref):
    out_ref[...] = (extra_refs[0][...].astype(jnp.float32) + totals[0]).astype(jnp.bfloat16)


def begin_kernel(device_ref, in_ref, out_ref):
    out_ref[...] = in_ref[...]


def attend_kernel(scale, query_ref, key_ref, value_ref, limit_ref, out_ref):
    heads, rows, head_dim = query_ref.shape
    span = key_ref.shape[0]
    value_heads = key_ref.shape[1] // head_dim
    group = heads // value_heads
    devices = out_ref.shape[0]
    pairs = heads * rows // devices
    place = lax.broadcasted_iota(jnp.int32, (rows, span), 1)
    visible = (place < limit_ref[:, :1])[None]
    for g in range(value_heads):
        lanes = pl.ds(g * head_dim, head_dim)
        queries = query_ref[g * group : (g + 1) * group].reshape(group * rows, head_dim)
        logits = lax.dot_general(
            queries, key_ref[:, lanes], (((1,), (1,)), ((), ())),
            preferred_element_type=jnp.float32,
        ) * scale
        masked = jnp.where(visible, logits.reshape(group, rows, span), MASKED)
        top = jnp.max(masked, axis=2, keepdims=True)
        weights = jnp.where(visible, jnp.exp(masked - top), 0.0)
        total = jnp.sum(weights, axis=2, keepdims=True).reshape(group * rows, 1)
        top = top.reshape(group * rows, 1)
        summed = jnp.dot(
            weights.astype(jnp.bfloat16).reshape(group * rows, span), value_ref[:, lanes],
            preferred_element_type=jnp.float32,
        )
        seen = total > 0.0
        safe = jnp.where(seen, total, 1.0)
        means = (summed / safe).astype(jnp.bfloat16)
        level = jnp.where(seen, top + jnp.log(safe), MASKED)
        across = jnp.transpose(jnp.broadcast_to(level, (group * rows, LANES)))[:8]
        for first in range(0, group * rows, LANES):
            line = across[:, first : first + LANES]
            high = line.astype(jnp.bfloat16)
            rest = line - high.astype(jnp.float32)
            middle = rest.astype(jnp.bfloat16)
            low = (rest - middle.astype(jnp.float32)).astype(jnp.bfloat16)
            row = lax.broadcasted_iota(jnp.int32, line.shape, 0)
            terms = jnp.where(
                row == 0,
                high.astype(jnp.float32),
                jnp.where(row == 1, middle.astype(jnp.float32), low.astype(jnp.float32)),
            ).astype(jnp.bfloat16)
            for begin in range(0, LANES, pairs):
                index = (g * group * rows + first + begin) // pairs
                out_ref[index, :pairs] = means[first + begin : first + begin + pairs]
                out_ref[index, pairs:] = terms


def terms_of(level):
    line = jnp.transpose(level)[:8]
    high = line.astype(jnp.bfloat16).astype(jnp.float32)
    rest = line - high
    middle = rest.astype(jnp.bfloat16).astype(jnp.float32)
    row = lax.broadcasted_iota(jnp.int32, line.shape, 0)
    return jnp.where(row == 0, high, jnp.where(row == 1, middle, rest - middle)).astype(jnp.bfloat16)


def read_message(message):
    pairs = message.shape[0] - 8
    terms = message[pairs:].astype(jnp.float32)
    line = terms[0:1] + terms[1:2] + terms[2:3]
    return message[:pairs].astype(jnp.float32), jnp.transpose(jnp.broadcast_to(line, (LANES, LANES)))


def merge(parts):
    peak = parts[0][1]
    for _, level in parts[1:]:
        peak = jnp.maximum(peak, level)
    shares = [jnp.exp(level - peak) for _, level in parts]
    denominator = sum(shares[1:], shares[0])
    numerator = shares[0] * parts[0][0]
    for share, (mean, _) in zip(shares[1:], parts[1:]):
        numerator = numerator + share * mean
    return numerator / denominator, peak + jnp.log(denominator)


def put_message(message_ref, mean, level):
    pairs = mean.shape[0]
    message_ref[:pairs] = mean.astype(jnp.bfloat16)
    message_ref[pairs:] = terms_of(level)


def attend_unit_kernel(scale, head_dim, sends, device_ref, blocks_ref, key_ref, value_ref, limit_ref, *out_refs):
    value_heads, rows, _ = blocks_ref.shape
    span = value_ref.shape[0]
    local = LANES // (value_heads * rows)
    count = local * rows
    heads = value_heads * local
    group_index = lax.div(device_ref[0], lax.axis_size("ctx") // value_heads)
    limit = limit_ref[:, :1]
    visible = (lax.broadcasted_iota(jnp.int32, (rows, span), 1) < limit)[None]
    seen = jnp.broadcast_to((limit > 0)[None], (heads, rows, 1)).reshape(heads * rows, 1)
    logits = []
    for g in range(value_heads):
        block = blocks_ref[lax.bitwise_xor(group_index, g)]
        queries = jnp.concatenate(
            [block[:, h * head_dim : (h + 1) * head_dim] for h in range(local)], axis=0
        )
        logits.append(
            jnp.dot(
                queries, key_ref[g * head_dim : (g + 1) * head_dim, :],
                preferred_element_type=jnp.float32,
            )
        )
    logits = jnp.concatenate(logits, axis=0).reshape(heads, rows, span)
    masked = jnp.where(visible, logits, MASKED)
    top = jnp.max(masked, axis=2, keepdims=True)
    weights = jnp.exp2((masked - top) * (scale * math.log2(math.e)))
    total = jnp.sum(weights, axis=2, keepdims=True).reshape(heads * rows, 1)
    rounded = weights.astype(jnp.bfloat16).reshape(heads * rows, span)
    summed = jnp.concatenate(
        [
            jnp.dot(
                rounded[g * count : (g + 1) * count],
                value_ref[:, g * head_dim : (g + 1) * head_dim],
                preferred_element_type=jnp.float32,
            )
            for g in range(value_heads)
        ],
        axis=0,
    )
    mean = summed / total
    level = jnp.where(seen, top.reshape(heads * rows, 1) * scale + jnp.log(total), MASKED)
    level = jnp.broadcast_to(level, (heads * rows, LANES))
    if sends:
        put_message(out_refs[0], mean, level)
    else:
        out_refs[0][...] = mean
        out_refs[1][...] = level


def merge_pair_kernel(mean_ref, level_ref, message_ref, sent_ref):
    mean, level = merge([(mean_ref[...], level_ref[...]), read_message(message_ref[...])])
    put_message(sent_ref, mean, level)


def merge_next_kernel(mean_ref, level_ref, core_ref, message_ref, sent_ref, mean_out_ref, level_out_ref):
    mean, level = merge(
        [(mean_ref[...], level_ref[...]), read_message(core_ref[...]), read_message(message_ref[...])]
    )
    put_message(sent_ref, mean, level)
    mean_out_ref[...] = mean
    level_out_ref[...] = level


def fresh_kernel(
    scale, head_dim, value_heads, key_width, device_ref, held_ref, brought_ref, far_ref, far_brought_ref,
    score_ref, value_ref,
):
    _, rows, used = far_ref.shape
    query_width = used - 2 * key_width
    run = head_dim // key_width
    group_index = lax.div(device_ref[0], run)
    core = lax.rem(device_ref[0], 2)
    step = lax.rem(lax.div(device_ref[0], 2), 2)
    for g in range(value_heads):
        turned = lax.bitwise_xor(group_index, g)
        news = []
        for index in range(run):
            same = core == index % 2
            block = jnp.where(
                step == index // 2,
                jnp.where(same, held_ref[turned], far_ref[turned]),
                jnp.where(same, brought_ref[turned], far_brought_ref[turned]),
            )
            news.append(block[:, query_width:])
        key = jnp.concatenate([new[:, :key_width] for new in news], axis=1).astype(jnp.float32)
        value = jnp.concatenate([new[:, key_width:] for new in news], axis=1).astype(jnp.float32)
        queries = far_brought_ref[turned]
        for h in range(query_width // head_dim):
            query = queries[:, h * head_dim : (h + 1) * head_dim].astype(jnp.float32)
            score = jnp.sum(query * key, axis=1, keepdims=True) * scale
            span = pl.ds((g * (query_width // head_dim) + h) * rows, rows)
            score_ref[span, :] = jnp.broadcast_to(score, (rows, LANES))
            value_ref[span, :] = value


def settle_kernel(
    rows, mean_ref, level_ref, *refs
):
    *message_refs, score_ref, value_ref, out_ref = refs
    parts = [(mean_ref[...], level_ref[...])]
    parts += [read_message(message_ref[...]) for message_ref in message_refs]
    parts.append((value_ref[...], score_ref[...]))
    mean, _ = merge(parts)
    done = mean.astype(jnp.bfloat16)
    owners, _, width = out_ref.shape
    local = width // LANES
    for g in range(owners):
        first = g * local * rows
        out_ref[g] = jnp.concatenate(
            [done[first + h * rows : first + (h + 1) * rows] for h in range(local)], axis=1
        )


def residual_finish(factor, totals, extra_refs, out_ref):
    out_ref[...] = (extra_refs[0][...].astype(jnp.float32) + totals[0]).astype(jnp.bfloat16)


def by_group(device, place_index, devices):
    (stride, groups, _), (step, _, _), _ = digits(devices)
    place_in_group = lax.bitwise_xor(lax.rem(device, stride), step + 1)
    far = lax.div(place_index, devices // 2) if not isinstance(place_index, int) else place_index // (devices // 2)
    near_place = lax.rem(place_index, devices // 2)
    turned = lax.bitwise_xor(place_in_group, lax.div(near_place, groups) * step)
    return lax.rem(near_place, groups) * stride + lax.bitwise_xor(turned, far)


def order_kernel(device_ref, held_ref, out_ref):
    devices = held_ref.shape[0]

    def move(owner, carry):
        place = place_of(lax.bitwise_xor(device_ref[0], owner), devices)
        out_ref[owner] = held_ref[place]
        return carry

    lax.fori_loop(0, devices, move, 0, unroll=4)


def table_kernel(cos_ref, sin_ref, cos_out_ref, sin_out_ref):
    lane = lax.broadcasted_iota(jnp.int32, sin_ref.shape, 1)
    cos_out_ref[...] = cos_ref[...]
    sin_out_ref[...] = jnp.where(lane % 2 == 1, sin_ref[...], -sin_ref[...])


def finish_kernel(numerator_ref, denominator_ref, out_ref):
    out_ref[...] = (numerator_ref[...] / denominator_ref[...]).astype(jnp.bfloat16)


def output_kernel(blocks_ref, weight_ref, residual_ref, mid_ref, total):
    heads, _, head_dim = blocks_ref.shape
    total[...] = jnp.zeros_like(total)

    def step(index, carry):
        block = jnp.concatenate([blocks_ref[2 * index], blocks_ref[2 * index + 1]], axis=1)
        span = pl.ds(pl.multiple_of(index * 2 * head_dim, head_dim), 2 * head_dim)
        total[...] += jnp.dot(block, weight_ref[span, :], preferred_element_type=jnp.float32)
        return carry

    lax.fori_loop(0, heads // 2, step, 0, unroll=4)
    mid_ref[...] = (residual_ref[...].astype(jnp.float32) + total[...]).astype(jnp.bfloat16)


def rotation(first_col, width, positions, head_dim):
    col = jnp.arange(width, dtype=jnp.int32)
    in_head = ((first_col + col - col % 2) % head_dim).astype(jnp.float32)
    frequency = jnp.exp(-(in_head / head_dim) * jnp.log(jnp.float32(ROPE_BASE)))
    angles = positions.astype(jnp.float32)[:, None] * frequency[None, :]
    return jnp.cos(angles), jnp.sin(angles)


def shards(
    hidden_in,
    attn_gain,
    w_query,
    w_key,
    w_value,
    rotated_prefix_keys,
    cache_values,
    w_out,
    ffn_gain,
    w_gate,
    w_up,
    w_down,
    doc_offsets,
    slot_request,
):
    devices = lax.axis_size("ctx")
    device = lax.axis_index("ctx")
    own = lax.optimization_barrier(device.astype(jnp.int32)[None])
    rows, width = hidden_in.shape
    span, value_heads, head_dim = rotated_prefix_keys.shape
    query_width = w_query.shape[1]
    key_width = w_key.shape[1]
    heads = query_width * devices // head_dim
    group = heads // value_heads
    scale = 1.0 / math.sqrt(head_dim)
    slot_index = jnp.arange(rows, dtype=jnp.int32)
    positions = jnp.sum(
        jnp.where(slot_request[:, None] == slot_index[None, :], doc_offsets[None, :], 0), axis=1
    )

    def buffer(*shape, dtype=jnp.bfloat16):
        return jax.ShapeDtypeStruct(shape, dtype)

    def totals(*widths):
        return [pltpu.VMEM((rows, w), jnp.float32) for w in widths]

    used = query_width + 2 * key_width
    padded = -(-used // LANES) * LANES
    query_cos, query_sin = rotation(own * query_width, query_width, positions, head_dim)
    key_cos, key_sin = rotation(own * key_width, key_width, positions, head_dim)
    still = jnp.ones((rows, padded - query_width - key_width), jnp.float32)
    cosine = jnp.concatenate([query_cos, key_cos, still], axis=1)
    sine = jnp.concatenate([query_sin, key_sin, still * 0.0], axis=1)
    table = buffer(rows, padded, dtype=jnp.float32)
    cosine, sine = call(table_kernel, "table", (table, table), (cosine, sine), (), FLOPS["table"])
    begun = call(begin_kernel, "begin", buffer(rows, width), (own, hidden_in))
    sides = (w_key, w_value)
    if width % LANES == 0:
        sides = (w_key.T, w_value.T)
    projected = contract(
        "project", gathered(begun, hidden_in), own, (w_query, *sides), (query_width, key_width, key_width),
        attn_gain, project_finish, (cosine, sine), buffer(rows, used),
    )
    limit = jnp.broadcast_to((positions - own * span)[:, None], (rows, LANES))
    keys = rotated_prefix_keys.reshape(span, value_heads * head_dim)
    values = cache_values.reshape(span, value_heads * head_dim)
    rounds = digits(devices)
    if (
        len(rounds) == 3
        and rounds[0][1] == value_heads
        and rounds[1][1] == 2
        and head_dim == LANES
        and value_heads * (query_width // head_dim) * rows == LANES
    ):
        held, far, brought, far_brought = gathered(projected)
        unit = (LANES, LANES)
        message = buffer(LANES + 8, LANES)
        wide = buffer(*unit, dtype=jnp.float32)
        work = heads * rows * span * head_dim
        keys_across = rotated_prefix_keys.transpose(1, 2, 0).reshape(value_heads * head_dim, span)

        late_limit = call(begin_kernel, "hold", buffer(rows, LANES, dtype=jnp.int32), (own, limit))

        def attended(label, blocks, sends, limit=limit):
            return call(
                lambda *refs: attend_unit_kernel(scale, head_dim, sends, *refs), "attend_" + label,
                message if sends else (wide, wide), (own, blocks, keys_across, values, limit), (), work,
            )

        given = attended("a", held, True)
        taken = shifted(given, 1)
        given = call(merge_pair_kernel, "merge_core", message, (*attended("b", far, False), taken))
        taken_next = shifted(given, rounds[1][0])
        given = attended("c", brought, True, late_limit)
        taken = shifted(given, 1)
        mean, level = attended("d", far_brought, False, late_limit)
        given, mean, level = call(
            merge_next_kernel, "merge_next", (message, wide, wide), (mean, level, taken, taken_next)
        )
        taken = []
        for digit in range(1, rounds[0][1]):
            taken.append(shifted(given, rounds[0][0] * digit))
        score, value = call(
            lambda *refs: fresh_kernel(scale, head_dim, value_heads, key_width, *refs), "fresh",
            (wide, wide), (own, held, brought, far, far_brought),
        )
        done = call(
            lambda *refs: settle_kernel(rows, *refs), "settle",
            buffer(value_heads, rows, query_width), (mean, level, *taken, score, value),
        )
        mid_part = contract(
            "output", pieces_of(done, *rounds[1][:2]), own, (w_out,), (width,),
            None, residual_finish, (hidden_in,), buffer(rows, width), by_group,
        )
    else:
        packed = exchange(jnp.broadcast_to(projected[None], (devices, rows, used)))

        def unpacked(first, part_width):
            part = packed[:, :, first : first + part_width]
            if part_width >= head_dim:
                split = part.reshape(devices, rows, part_width // head_dim, head_dim)
                return split.transpose(0, 2, 1, 3).reshape(-1, rows, head_dim)
            run = head_dim // part_width
            return part.reshape(-1, run, rows, part_width).transpose(0, 2, 1, 3).reshape(
                -1, rows, head_dim
            )

        queries = unpacked(0, query_width)
        key_new = unpacked(query_width, key_width)
        value_new = unpacked(query_width + key_width, key_width)
        pairs = heads * rows // devices
        sent = call(
            lambda *refs: attend_kernel(scale, *refs), "attend", buffer(devices, pairs + 8, LANES),
            (
                queries,
                keys,
                values,
                limit,
            ),
            (),
            4 * heads * rows * span * head_dim,
        )
        got = exchange(sent)
        first_pair = device * pairs
        means = got[:, :pairs].astype(jnp.float32)
        terms = lax.dynamic_slice_in_dim(
            got[:, pairs : pairs + 3].astype(jnp.float32), first_pair % LANES, pairs, 2
        )
        levels = terms[:, 0] + terms[:, 1] + terms[:, 2]

        def mine(every):
            return lax.dynamic_slice_in_dim(
                every.reshape(heads * rows, head_dim), first_pair, pairs, 0
            ).astype(jnp.float32)

        def spread(new):
            return jnp.broadcast_to(new[:, None], (value_heads, group, rows, head_dim))

        own_score = jnp.sum(mine(queries) * mine(spread(key_new)), axis=1) * scale
        own_value = mine(spread(value_new))
        peak = jnp.maximum(jnp.max(levels, axis=0), own_score)
        shares = jnp.exp(levels - peak[None, :])
        own_share = jnp.exp(own_score - peak)
        numerator = jnp.sum(shares[..., None] * means, axis=0) + own_share[:, None] * own_value
        denominator = jnp.sum(shares, axis=0) + own_share
        attn_part = call(
            finish_kernel, "finish", buffer(pairs, head_dim), (numerator, denominator[:, None]), (),
            FLOPS["finish"],
        )
        held = together(gathered(attn_part))
        attn_all = call(
            order_kernel, "order", buffer(devices, pairs, head_dim), (own, held)
        )
        mid_part = call(
            output_kernel, "output", buffer(rows, width),
            (attn_all.reshape(heads, rows, head_dim), w_out, hidden_in),
            totals(width),
            2 * rows * heads * head_dim * width,
        )
    hidden_width = w_gate.shape[1]
    hidden = contract(
        "gated", gathered(mid_part), own, (w_gate, w_up), (hidden_width, hidden_width),
        ffn_gain, gated_finish, (), buffer(rows, hidden_width),
    )
    hidden = call(begin_kernel, "relay", buffer(rows, hidden_width), (own, hidden))
    return contract(
        "down", gathered(hidden), own, (w_down,), (width,),
        None, down_finish, (mid_part,), buffer(rows, width),
    )


def solution(mesh):
    return jax.shard_map(
        shards,
        mesh=mesh,
        in_specs=(
            P("groups", "ctx"),
            P(),
            P(None, "ctx"),
            P(None, "ctx"),
            P(None, "ctx"),
            P(("groups", "ctx"), None, None),
            P(("groups", "ctx"), None, None),
            P(None, "ctx"),
            P(),
            P(None, "ctx"),
            P(None, "ctx"),
            P(None, "ctx"),
            P("groups"),
            P("groups"),
        ),
        out_specs=P("groups", "ctx"),
        check_vma=False,
    )
```
